128 devices in a mesh: gx: 16 (over z, x), gy: 8 (over y, core).
Axes of the slice: x: 4, y: 4, z: 4, core: 2. Of those that a mesh axis runs over, the one named last changes fastest.
Arguments:
- cotangent: float32 [16, 8, 42, 1024], P('gx', 'gy'), may hold values from -6 to 6
- section_states: bfloat16 [3, 16, 8, 42, 1024], P(None, 'gx', 'gy'), may hold values from -6 to 6
- inverse_area: float32 [16, 8, 1024], P('gx', 'gy'), may hold values from 0.5 to 2
- edge_length: float32 [16, 8, 3, 1024], P('gx', 'gy'), may hold values from 0.5 to 1.5
- roughness: float32 [16, 8, 1024], P('gx', 'gy'), may hold values from 0.5 to 2
- soil_conductance: float32 [16, 8, 1024], P('gx', 'gy'), may hold values from 0.5 to 2
- zone_friction: float32 [512], replicated, may hold values from 0.25 to 1
- zone_conductivity: float32 [512], replicated, may hold values from 0.25 to 1
- wet_mask: int32 [16, 8, 1024], P('gx', 'gy'), may hold values 0 or 1
- element_zone: int32 [16, 8, 1024], P('gx', 'gy'), may hold values from 0 to 511, as said below
- send_face: int32 [16, 8, 8, 256], P('gx', 'gy'), may hold values from 0 to 3071, as said below
- send_count: int32 [16, 8, 8], P('gx', 'gy'), may hold values from 0 to 256, as said below
- face_partner: int32 [16, 8, 3, 1024], P('gx', 'gy'), may hold values from 0 to 4867, as said below
- volume_matrix: float32 [12, 12], replicated, may hold values from -1.75 to 1.75
- flux_in: float32 [8, 8], replicated, may hold values from -2 to 2
- flux_out: float32 [8, 8], replicated, may hold values from -2 to 2
Outputs:
- adjoint: float32 [16, 8, 42, 1024], P('gx', 'gy')
- zone_grads: float32 [2, 512], replicated
The draws below stay inside these ranges and needn't reach their ends.
Inputs may be any that keep to these rules, and one draw needn't show every extreme that they name: `element_zone`: zones lie near their partition: an element of partition (a, b) has a zone among the 8 zones from (a*8+b)*4 on, modulo 512. send_count[a, b, n] equals send_count of the partition at offset n for offset 7 - n; it is 0 where that partition lies outside the grid, 1 to 4 for the four diagonal offsets (4 for some pair in every draw), at least 192 for the others, and 256 for some pair in every draw. `send_face`: the live slots of a partition name distinct faces; slots at or beyond the count hold 0. `face_partner`: the faces are paired: a face sent in slot j to offset n faces entry 3072 + n*256 + j, the other faces face a local face whose partner they are, or themselves.
All inputs are finite; a program needn't handle non-finite values. No bound on the sum of `wet_mask` on one device may be relied on, other than what follows from the above.
Results may differ from the reference program's by a relative error of at most 0.0003.
Values may be sent and summed in bfloat16 or wider, within the bound.
A program may use at most 64 MiB of HBM per device.

```python
import math
import jax
import jax.numpy as jnp
import numpy as np
from jax import lax

LAYERS = 10
E_DEV = 1024
CAP = 256
ZONE_DEV = 4
GRID_X = 16
GRID_Y = 8
ZONES = 512
STATE_ROWS = 42


def neighbour_counts(key):
    key_x, key_y, key_pick, key_one, key_two = jax.random.split(key, 5)
    least_count = 3 * CAP // 4
    along_x = jax.random.randint(key_x, (GRID_X - 1, GRID_Y), least_count, CAP + 1)
    forced_pair = jax.random.randint(key_pick, (), 0, (GRID_X - 1) * GRID_Y)
    along_x = along_x.reshape(-1).at[forced_pair].set(CAP).reshape(GRID_X - 1, GRID_Y)
    along_y = jax.random.randint(key_y, (GRID_X, GRID_Y - 1), least_count, CAP + 1)
    diag_one = jax.random.randint(key_one, (GRID_X - 1, GRID_Y - 1), 1, 5)
    diag_one = diag_one.at[0, 0].set(4)
    diag_two = jax.random.randint(key_two, (GRID_X - 1, GRID_Y - 1), 1, 5)
    pad_x = jnp.pad(along_x, ((1, 1), (0, 0)))
    pad_y = jnp.pad(along_y, ((0, 0), (1, 1)))
    pad_one = jnp.pad(diag_one, ((1, 1), (1, 1)))
    pad_two = jnp.pad(diag_two, ((1, 1), (1, 1)))
    counts = jnp.stack([pad_one[:-1, :-1], pad_x[:-1], pad_two[:-1, 1:], pad_y[:, :-1], pad_y[:, 1:], pad_two[1:, :-1], pad_x[1:], pad_one[1:, 1:]], axis=-1)
    return counts.astype(jnp.int32)


def partition_tables(key, counts):
    face_total = 3 * E_DEV
    middle = (jax.random.permutation(key, face_total - 2) + 1).astype(jnp.int32)
    ordering = jnp.concatenate([jnp.full((1,), face_total - 1, jnp.int32), middle, jnp.zeros((1,), jnp.int32)])
    upper_bound = jnp.cumsum(counts).astype(jnp.int32)
    lower_bound = upper_bound - counts
    total_sent = upper_bound[-1]
    slot_index = jnp.arange(CAP, dtype=jnp.int32)
    outgoing = jnp.where(slot_index[None, :] < counts[:, None], ordering[jnp.clip(lower_bound[:, None] + slot_index[None, :], 0, face_total - 1)], 0)
    positions = jnp.arange(face_total, dtype=jnp.int32)
    direction = jnp.minimum(jnp.sum((positions[:, None] >= upper_bound[None, :]).astype(jnp.int32), axis=1), 7)
    remote = 3 * E_DEV + direction * CAP + positions - lower_bound[direction]
    shifted = positions - total_sent
    partner_position = total_sent + jnp.bitwise_xor(shifted, 1)
    inside = partner_position < face_total
    local_partner = jnp.where(inside, ordering[jnp.clip(partner_position, 0, face_total - 1)], ordering)
    values = jnp.where(positions < total_sent, remote, local_partner).astype(jnp.int32)
    partner = jnp.zeros((face_total,), jnp.int32).at[ordering].set(values)
    return (outgoing.astype(jnp.int32), partner.reshape(3, E_DEV))


def mesh_tables(key):
    base_key = jax.random.fold_in(key, 31)
    counts = neighbour_counts(jax.random.fold_in(base_key, 1))
    device_keys = jax.random.split(jax.random.fold_in(base_key, 2), GRID_X * GRID_Y)
    outgoing, partner = jax.vmap(partition_tables)(device_keys, counts.reshape(GRID_X * GRID_Y, 8))
    return (counts, outgoing.reshape(GRID_X, GRID_Y, 8, CAP), partner.reshape(GRID_X, GRID_Y, 3, E_DEV))


def draw_send_count(key, part):
    return mesh_tables(key)[0]


def draw_send_face(key, part):
    return mesh_tables(key)[1]


def draw_face_partner(key, part):
    return mesh_tables(key)[2]


def draw_element_zone(key, part):
    offsets = jax.random.randint(jax.random.fold_in(key, 23), (GRID_X, GRID_Y, E_DEV), 0, 2 * ZONE_DEV)
    device_number = jnp.arange(GRID_X, dtype=jnp.int32)[:, None] * GRID_Y + jnp.arange(GRID_Y, dtype=jnp.int32)[None, :]
    return ((device_number[:, :, None] * ZONE_DEV + offsets) % ZONES).astype(jnp.int32)


def with_ends(entries, rng, smallest, largest):
    dims = entries.shape
    place = [jax.random.randint(jax.random.fold_in(rng, axis), (), 0, dims[axis]) for axis in range(len(dims))]
    entries = entries.at[tuple(place)].set(smallest)
    longest = dims.index(max(dims))
    place[longest] = (place[longest] + 1) % dims[longest]
    return entries.at[tuple(place)].set(largest)


def level_of(own_key, shape, cuts, least, largest):
    gain, own = 1.0, jax.random.fold_in(own_key, 6)
    for axis_at, parts in cuts:
        draws = jnp.exp(jax.random.uniform(jax.random.fold_in(own, axis_at), (parts,), jnp.float32, least / len(cuts), largest / len(cuts)))
        gain = gain * jnp.repeat(draws, shape[axis_at] // parts).reshape([-1 if axis == axis_at else 1 for axis in range(len(shape))])
    return gain


def gaussian(own_key, shape, spread, limit, cuts=(), kind=jnp.bfloat16):
    gain = level_of(own_key, shape, cuts, -0.22, 0.18) if cuts else 1.0
    values = jax.random.normal(own_key, shape, jnp.float32) * spread * gain
    return jnp.minimum(jnp.maximum(values, -limit), limit).astype(kind)


def setup_inputs(seed: int = 0) -> dict:
    seeds = jax.random.split(jax.random.key(seed), 17)
    cotangent = gaussian(seeds[0], (GRID_X, GRID_Y, STATE_ROWS, E_DEV), 1.0, 6.0, ((0, 16), (1, 8)), jnp.float32)
    section_states = gaussian(seeds[1], (3, GRID_X, GRID_Y, STATE_ROWS, E_DEV), 1.0, 6.0, ((1, 16), (2, 8)))
    inverse_area = jnp.clip(jnp.exp(math.log(2.0) - 1.3862944 * jax.random.uniform(seeds[2], (GRID_X, GRID_Y, E_DEV), jnp.float32) ** level_of(seeds[2], (GRID_X, GRID_Y, E_DEV), ((0, 16), (1, 8)), -0.2, 0.2)), 0.5, 2.0)
    edge_length = jnp.clip(jnp.exp(math.log(1.5) - 1.0986123 * jax.random.uniform(seeds[3], (GRID_X, GRID_Y, 3, E_DEV), jnp.float32) ** level_of(seeds[3], (GRID_X, GRID_Y, 3, E_DEV), ((0, 16), (1, 8)), -0.2, 0.2)), 0.5, 1.5)
    roughness = jnp.clip(jnp.exp(math.log(2.0) - 1.3862944 * jax.random.uniform(seeds[4], (GRID_X, GRID_Y, E_DEV), jnp.float32) ** level_of(seeds[4], (GRID_X, GRID_Y, E_DEV), ((0, 16), (1, 8)), -0.2, 0.2)), 0.5, 2.0)
    soil_conductance = jnp.clip(jnp.exp(math.log(2.0) - 1.3862944 * jax.random.uniform(seeds[5], (GRID_X, GRID_Y, E_DEV), jnp.float32) ** level_of(seeds[5], (GRID_X, GRID_Y, E_DEV), ((0, 16), (1, 8)), -0.2, 0.2)), 0.5, 2.0)
    zone_friction = jnp.clip(jnp.exp(jax.random.uniform(seeds[6], (ZONES,), jnp.float32, math.log(0.25), math.log(1.0))), 0.25, 1.0)
    zone_conductivity = jnp.clip(jnp.exp(jax.random.uniform(seeds[7], (ZONES,), jnp.float32, math.log(0.25), math.log(1.0))), 0.25, 1.0)
    wet_mask = with_ends((jax.random.randint(seeds[8], (GRID_X, GRID_Y, E_DEV), 0, 4) < 3).astype(jnp.int32), jax.random.fold_in(seeds[8], 1), 0, 1)
    element_zone = draw_element_zone(jax.random.fold_in(seeds[16], 71), 0)
    send_face = draw_send_face(jax.random.fold_in(seeds[16], 71), 0)
    send_count = draw_send_count(jax.random.fold_in(seeds[16], 71), 0)
    face_partner = draw_face_partner(jax.random.fold_in(seeds[16], 71), 0)
    volume_matrix = gaussian(seeds[13], (12, 12), 12 ** -0.5, 1.75, (), jnp.float32)
    flux_in = gaussian(seeds[14], (8, 8), 8 ** -0.5, 2.0, (), jnp.float32)
    flux_out = gaussian(seeds[15], (8, 8), 8 ** -0.5, 2.0, (), jnp.float32)
    return dict(cotangent=cotangent, section_states=section_states, inverse_area=inverse_area, edge_length=edge_length, roughness=roughness, soil_conductance=soil_conductance, zone_friction=zone_friction, zone_conductivity=zone_conductivity, wet_mask=wet_mask, element_zone=element_zone, send_face=send_face, send_count=send_count, face_partner=face_partner, volume_matrix=volume_matrix, flux_in=flux_in, flux_out=flux_out)


TIME_STEP = 0.2
SALT_RETURN = 0.5
LATERAL = 0.5
GRAD_WEIGHT = 1.0 / 64.0
FACE_NODES = ((1, 2), (2, 0), (0, 1))
DIRECTIONS = ((-1, -1), (-1, 0), (-1, 1), (0, -1), (0, 1), (1, -1), (1, 0), (1, 1))
MOMENTUM_ROWS = np.array([0, 0, 0, 1, 1, 1, 1, 1, 1, 0, 0, 0], np.float32)

def trace_rows():
    channels = 8 + 2 * LAYERS
    rows = np.zeros((channels, 3), np.int32)
    for face_no in range(3):
        for end_no in range(2):
            node_no = FACE_NODES[face_no][end_no]
            for comp_no in range(4):
                rows[comp_no * 2 + end_no, face_no] = comp_no * 3 + node_no
            for layer_no in range(LAYERS):
                rows[8 + layer_no * 2 + end_no, face_no] = 12 + layer_no * 3 + node_no
    return rows.reshape(-1)

def take_traces(state, rows):
    channels = rows.shape[0] // 3
    return state[rows].reshape(channels, 3 * state.shape[1])

def lift_back(flux, rows, row_count):
    return jnp.zeros((row_count, flux.shape[-1]), jnp.float32).at[rows].add(flux)

def send_block(flat_traces, send_face, send_count):
    slot_index = jnp.arange(send_face.shape[1])
    live_slots = (slot_index[None, :] < send_count[:, None]).astype(jnp.float32)
    return flat_traces[:, send_face] * live_slots[None]

def section_speed(flat_traces, outer_flat):
    return jnp.sqrt(1.0 + 0.25 * lax.optimization_barrier(jnp.mean(flat_traces[:8] ** 2 + outer_flat[:8] ** 2, axis=0)))

def local_operator(state, received, conductivity, friction, wave_speed, inverse_area, edge_length, wet_mask, partner, volume_matrix, flux_in, flux_out, rows):
    element_count = state.shape[1]
    channels = rows.shape[0] // 3
    flat_traces = take_traces(state, rows)
    trace_table = jnp.concatenate([flat_traces, received.reshape(channels, -1)], axis=1)
    outer_traces = trace_table[:, partner.reshape(-1)].reshape(channels, 3, element_count)
    inner_traces = flat_traces.reshape(channels, 3, element_count)
    surf_inner = inner_traces[:8]
    surf_outer = outer_traces[:8]
    flux_surface = jnp.einsum('ab,bfe->afe', flux_in, surf_inner, precision=lax.Precision.HIGHEST) - jnp.einsum('ab,bfe->afe', flux_out, surf_outer, precision=lax.Precision.HIGHEST) + 0.5 * wave_speed[None] * (surf_inner - surf_outer)
    flux_pore = LATERAL * conductivity[None, None] * (outer_traces[8:] - inner_traces[8:])
    flux_all = jnp.concatenate([flux_surface, flux_pore], axis=0) * edge_length[None]
    lifted = lift_back(flux_all.reshape(channels * 3, element_count), rows, state.shape[0])
    volume = jnp.dot(volume_matrix, state[:12], precision=lax.Precision.HIGHEST)
    top_exchange = conductivity[None] * (state[9:12] - state[12:15])
    momentum = jnp.asarray(MOMENTUM_ROWS, dtype=jnp.float32)[:, None]
    surface = inverse_area[None] * (volume + lifted[:12]) - momentum * friction[None] * state[:12]
    surface = jnp.concatenate([surface[:9], surface[9:12] - SALT_RETURN * top_exchange], axis=0) * wet_mask[None]
    layers = state[12:].reshape(LAYERS, 3, element_count)
    between = conductivity[None, None] * (layers[:-1] - layers[1:])
    from_above = jnp.concatenate([top_exchange[None], between], axis=0)
    to_below = jnp.concatenate([between, jnp.zeros((1, 3, element_count), jnp.float32)], axis=0)
    pore = (from_above - to_below).reshape(3 * LAYERS, element_count) + inverse_area[None] * lifted[12:]
    return jnp.concatenate([surface, pore], axis=0)

def route_whole(blocks):
    size_x = blocks.shape[0]
    size_y = blocks.shape[1]
    padded = jnp.pad(blocks, ((1, 1), (1, 1), (0, 0), (0, 0), (0, 0)))
    pieces = []
    for dir_no in range(8):
        step_x, step_y = DIRECTIONS[dir_no]
        pieces.append(padded[1 + step_x:1 + step_x + size_x, 1 + step_y:1 + step_y + size_y, :, 7 - dir_no])
    return jnp.stack(pieces, axis=3)

def grid_map(function):
    return jax.vmap(jax.vmap(function))

def reference(cotangent, section_states, inverse_area, edge_length, roughness, soil_conductance, zone_friction, zone_conductivity, wet_mask, element_zone, send_face, send_count, face_partner, volume_matrix, flux_in, flux_out):
    rows = jnp.asarray(trace_rows(), dtype=jnp.int32)
    channels = rows.shape[0] // 3
    wetness = wet_mask.astype(jnp.float32)
    traces_of = grid_map(lambda state: take_traces(state, rows))

    def blocks_of(flat_all):
        return grid_map(send_block)(flat_all, send_face, send_count)

    def outer_one(flat_traces, received, partner):
        return jnp.concatenate([flat_traces, received.reshape(channels, -1)], axis=1)[:, partner.reshape(-1)]

    def apply_one(state, received, conductivity, friction, wave_speed, area_one, edges_one, wet_one, partner):
        return local_operator(state, received, conductivity, friction, wave_speed, area_one, edges_one, wet_one, partner, volume_matrix, flux_in, flux_out, rows)
    apply_grid = grid_map(apply_one)

    def section_adjoint(section_no, weight_field):
        forward_state = section_states[section_no].astype(jnp.float32)
        flat_all = traces_of(forward_state)
        received = route_whole(blocks_of(flat_all))
        outer_all = grid_map(outer_one)(flat_all, received, face_partner)
        wave_speed = grid_map(section_speed)(flat_all, outer_all).reshape(forward_state.shape[0], forward_state.shape[1], 3, -1)
        moment = jnp.sqrt(1.0 + lax.optimization_barrier(jnp.mean(forward_state[:, :, 3:9] ** 2, axis=2)))

        def whole_operator(state, friction_zone, conduct_zone):
            conductivity = conduct_zone[element_zone] * soil_conductance
            friction = friction_zone[element_zone] * roughness * moment
            incoming = route_whole(blocks_of(traces_of(state)))
            return apply_grid(state, incoming, conductivity, friction, wave_speed, inverse_area, edge_length, wetness, face_partner)
        unused, pullback = jax.vjp(whole_operator, forward_state, zone_friction, zone_conductivity)
        state_bar, friction_bar, conduct_bar = pullback(TIME_STEP * weight_field)
        return (state_bar, jnp.stack([friction_bar, conduct_bar], axis=0))
    bar_two, grads_two = section_adjoint(2, cotangent)
    lam_two = 2.0 / 3.0 * (cotangent + bar_two)
    bar_one, grads_one = section_adjoint(1, lam_two)
    lam_one = 0.25 * (lam_two + bar_one)
    bar_zero, grads_zero = section_adjoint(0, lam_one)
    adjoint = cotangent / 3.0 + 0.75 * lam_two + lam_one + bar_zero
    zone_grads = GRAD_WEIGHT * (2.0 / 3.0 * grads_two + 0.25 * grads_one + grads_zero)
    return (adjoint, zone_grads)
```

```python
import jax
import jax.numpy as jnp
from jax import lax
from jax.experimental import pallas as pl
from jax.experimental.pallas import tpu as pltpu
from jax.sharding import PartitionSpec as P

GX, GY = 16, 8
COMPS = 14
QCOMP, ZCOMP = 14, 15
ZONES = 512
DT = 0.2
GRAD_WEIGHT = 1.0 / 64.0
FACE_NODES = ((1, 2), (2, 0), (0, 1))
MAIN = (1, 3, 4, 6)
DIAG = (0, 2, 5, 7)
STEPS = ((-1, -1), (-1, 0), (-1, 1), (0, -1), (0, 1), (1, -1), (1, 0), (1, 1))
WINDOW, BEHIND = 80, 36
MESH = pl.DeviceIdType.MESH
TILE = (8, 128)
F32 = jnp.float32


def take(x, idx):
    return jnp.take_along_axis(x, idx, axis=1, mode="promise_in_bounds")


def row(ref, *at):
    return jnp.broadcast_to(ref[at], TILE)


def pick(code, values, like):
    out = jnp.full(TILE, values[-1], like.dtype)
    for i in range(len(values) - 2, -1, -1):
        out = jnp.where(code == i, values[i], out)
    return out


def ends(nodes, is0, is1):
    a, b, c = nodes
    first = jnp.where(is0, b, jnp.where(is1, c, a))
    second = jnp.where(is0, c, jnp.where(is1, a, b))
    return first, second


def kernel(
    cot, states, area_ref, edge_ref, rough_ref, soil_ref, zf_ref, zc_ref, wet_ref, zone_ref, send_ref, partner_ref,
    vol, fin, fout,
    out, grads,
    tab, aux, xs, local, pre, lam, kept, sbuf, rbuf, sdiag, rdiag, cdiag, gyb, gxb,
    send_sem, recv_sem, gy_send, gy_recv, gx_send, gx_recv,
):
    ix, iy = lax.axis_index("gx"), lax.axis_index("gy")

    def at(dx, dy):
        return (lax.rem(ix + dx + GX, GX), lax.rem(iy + dy + GY, GY))

    barrier = pltpu.get_barrier_semaphore()
    peers = [at(*STEPS[n]) for n in DIAG]
    peers += [at(0, k) for k in range(1, GY)]
    peers += [at(k, 0) for k in range(1, GX)]
    for peer in peers:
        pl.semaphore_signal(barrier, inc=1, device_id=peer, device_id_type=MESH)

    sub = lax.broadcasted_iota(jnp.int32, TILE, 0)
    lane = lax.broadcasted_iota(jnp.int32, TILE, 1)

    area = area_ref[...]
    rough = rough_ref[...]
    wet = wet_ref[...].astype(F32)
    zone = zone_ref[...]
    edge = [edge_ref[f] for f in range(3)]
    kappa = jnp.zeros(TILE, F32)
    zfric = jnp.zeros(TILE, F32)
    zlo, zhi = zone & 127, zone >> 7
    for t in range(4):
        kappa = jnp.where(zhi == t, take(row(zc_ref, pl.ds(t, 1)), zlo), kappa)
        zfric = jnp.where(zhi == t, take(row(zf_ref, pl.ds(t, 1)), zlo), zfric)
    kappa = kappa * soil_ref[...]
    half_kappa = 0.5 * kappa
    rough_zone = zfric * rough

    slots = jnp.concatenate(
        [send_ref[n : n + 1, h * 128 : (h + 1) * 128] for n in MAIN for h in range(2)], axis=0
    )
    m_lo, m_hi, m_f = slots & 127, (slots >> 7) & 7, slots >> 10
    m_is0, m_is1 = m_f == 0, m_f == 1
    dslots = jnp.zeros(TILE, jnp.int32)
    for i, n in enumerate(DIAG):
        first = jnp.broadcast_to(send_ref[n : n + 1, 0:128], TILE)
        d = 3 - i
        moved = pltpu.roll(first, 4 * d, axis=1) if d else first
        dslots = jnp.where((lane >> 2) == d, moved, dslots)
    d_lo, d_hi, d_f = dslots & 127, (dslots >> 7) & 7, dslots >> 10
    d_is0, d_is1 = d_f == 0, d_f == 1

    p_lo, p_loc, p_rem, p_is0, p_is1 = [], [], [], [], []
    for f in range(3):
        p = partner_ref[f]
        there = p - 3072
        n = there >> 8
        slot_row = pick(n, (8, 0, 8, 2, 4, 8, 6, 8), p) + ((there >> 7) & 1)
        is_diag = (n == 0) | (n == 2) | (n == 5) | (n == 7)
        far = p >= 3072
        d_lane = pick(n, (0, 0, 4, 0, 0, 8, 0, 12), p) + (p & 3)
        p_lo.append(jnp.where(far & is_diag, d_lane, p & 127))
        p_loc.append(jnp.where(far, -1, (p >> 7) & 7))
        p_rem.append(jnp.where(far, jnp.where(is_diag, 8, slot_row), -1))
        p_is0.append((p >> 10) == 0)
        p_is1.append((p >> 10) == 1)

    def from_slots(ref, c):
        nodes = []
        for n in range(3):
            acc = jnp.zeros(TILE, F32)
            for s in range(8):
                acc = jnp.where(m_hi == s, take(row(ref, c * 3 + n, pl.ds(s, 1)), m_lo), acc)
            nodes.append(acc)
        return ends(nodes, m_is0, m_is1)

    def from_partner(ref, c, f):
        nodes = []
        for n in range(3):
            acc = jnp.zeros(TILE, F32)
            for s in range(8):
                acc = jnp.where(p_loc[f] == s, take(row(ref, c * 3 + n, pl.ds(s, 1)), p_lo[f]), acc)
            nodes.append(acc)
        return ends(nodes, p_is0[f], p_is1[f])

    def from_diag(ref):
        flat = ref.reshape(48 * 8, 128)
        halves = []
        for h in range(2):
            nodes = []
            for n in range(3):
                acc = jnp.zeros(TILE, F32)
                for s in range(8):
                    rows = flat[pl.ds((h * 24 + n) * 8 + s, 8, stride=24), :]
                    acc = jnp.where(d_hi == s, take(rows, d_lo), acc)
                nodes.append(acc)
            halves.append(ends(nodes, d_is0, d_is1))
        return halves

    for f in range(3):
        aux[FACE_NODES[f][0]] = edge[f]
        aux[3 + f] = half_kappa
    for r in range(6, 48):
        aux[r] = jnp.zeros(TILE, F32)
    for r in range(45, 48):
        tab[r] = zone.astype(F32)
    slot_edge = from_slots(aux, 0)[0]
    slot_kedge = from_slots(aux, 1)[0] * slot_edge
    d_aux = from_diag(aux)[0][0]
    d_edge = jnp.broadcast_to(d_aux[0:1], TILE)
    d_kedge = jnp.broadcast_to(d_aux[1:2], TILE) * d_edge
    d_scale = [jnp.where(sub < 4, d_edge, d_kedge), jnp.where(sub < 6, d_kedge, 1.0)]
    kept_ref = kept
    kedge = [half_kappa * edge[f] for f in range(3)]

    def copies(k):
        group = []
        for i, n in enumerate(MAIN):
            group.append((sbuf.at[k, i], rbuf.at[k, 3 - i], i, 3 - i, at(*STEPS[n])))
        for i, n in enumerate(DIAG):
            group.append((sdiag.at[k], rdiag.at[k, 3 - i], 4 + i, 4 + 3 - i, at(*STEPS[n])))
        return [
            pltpu.make_async_remote_copy(
                src_ref=src, dst_ref=dst, send_sem=send_sem.at[k, a], recv_sem=recv_sem.at[k, b],
                device_id=peer, device_id_type=MESH,
            )
            for src, dst, a, b, peer in group
        ]

    tf = jnp.zeros(TILE, F32)
    tc = jnp.zeros(TILE, F32)
    far_terms = [jnp.zeros(TILE, F32)] * 3
    started = []
    weights = {2: 2.0 / 3.0, 1: 0.25, 0: 1.0}
    for k in (2, 1, 0):
        v = cot if k == 2 else lam.at[k]
        weight = weights[k] * DT
        x = xs.at[k]
        xflat = x.reshape(42 * 8, 128)
        for s in range(8):
            xflat[pl.ds(s, 42, stride=8), :] = states[k, :, s * 128 : (s + 1) * 128].astype(F32)
        squares = []
        for n in range(3):
            squares.append(sum(x[c * 3 + n] * x[c * 3 + n] for c in range(4)))
        q = [squares[a] + squares[b] for a, b in FACE_NODES]
        for f in range(3):
            tab[42 + FACE_NODES[f][0]] = q[f]
        wet_area = wet * area
        for r in range(12):
            tab[r] = wet_area * v[r]
        for r in range(12, 42):
            tab[r] = area * v[r]

        last = ZCOMP if k == 2 else QCOMP
        for c in range(last + 1):
            pair = from_slots(tab, c)
            scale = slot_edge if c < 4 else slot_kedge
            for j in range(2 if c < COMPS else 1):
                value = pair[j] * scale if c < COMPS else pair[j]
                ch = c * 2 + j if c < COMPS else 28 + c - COMPS
                for d in range(4):
                    sbuf[k, d, ch] = value[2 * d : 2 * d + 2]
        halves = from_diag(tab)
        for h in range(2):
            for j in range(2):
                sdiag[k, j, h * 8 : h * 8 + 8] = halves[h][j] * d_scale[h]
        if k == 2:
            pl.semaphore_wait(barrier, len(peers))
        group = copies(k)
        for copy in group:
            copy.start()
        started += group

        if k == 2:
            for f in range(3):
                outer_edge = from_partner(aux, 0, f)[0]
                kept_ref[f] = outer_edge
                kept_ref[3 + f] = from_partner(aux, 1, f)[0] * outer_edge
        for f in range(3):
            for c in range(last + 1):
                pair = from_partner(tab, c, f)
                if c < COMPS:
                    scale = kept_ref[f] if c < 4 else kept_ref[3 + f]
                    local[f, c * 2] = pair[0] * scale
                    local[f, c * 2 + 1] = pair[1] * scale
                else:
                    local[f, 28 + c - COMPS] = pair[0]

        moment = jnp.sqrt(1.0 + (1.0 / 6.0) * sum(x[r] * x[r] for r in range(3, 9)))
        wet_friction = wet * rough_zone * moment
        acc = jnp.zeros(TILE, F32)
        for r in range(3, 9):
            acc = acc + v[r] * x[r]
        tf = tf - weight * (wet * rough * moment) * acc
        inner = [[None] * 8 for _ in range(3)]
        bars = [None] * 12
        for r in range(12):
            bars[r] = sum(vol[b, r] * tab[b] for b in range(12))
            if 3 <= r < 9:
                bars[r] = bars[r] - wet_friction * v[r]
        for f in range(3):
            for a in range(8):
                total = sum(
                    fin[b, a] * tab[(b // 2) * 3 + FACE_NODES[f][b % 2]] for b in range(8)
                )
                r = (a // 2) * 3 + FACE_NODES[f][a % 2]
                bars[r] = bars[r] + edge[f] * total
        own = jnp.zeros(TILE, F32)
        node_edge = [
            sum(kedge[f] for f in range(3) if n in FACE_NODES[f]) for n in range(3)
        ]
        for n in range(3):
            above = v[12 + n] - 0.5 * wet * v[9 + n]
            bars[9 + n] = bars[9 + n] + kappa * above
            own = own + kappa * above * (x[9 + n] - x[12 + n])
            for l in range(10):
                r = 12 + l * 3 + n
                below = v[r + 3] - v[r] if l < 9 else None
                if below is not None:
                    own = own + kappa * below * (x[r] - x[r + 3])
                    flow = kappa * (below - above)
                else:
                    flow = -kappa * above
                face = node_edge[n] * tab[r]
                own = own - face * x[r]
                pre[r] = flow - face
                above = below
        for r in range(12):
            pre[r] = bars[r]
        tc = tc + weight * own

        for copy in group:
            copy.wait_recv()
        for j in range(2):
            for h in range(2):
                acc = rdiag[k, 0, j, h * 8 : h * 8 + 8]
                for d in range(1, 4):
                    acc = jnp.where((lane >> 2) == d, rdiag[k, d, j, h * 8 : h * 8 + 8], acc)
                cdiag[j, h * 8 : h * 8 + 8] = acc

        def beyond(f, ch):
            acc = local[f, ch]
            for s in range(8):
                acc = jnp.where(
                    p_rem[f] == s, take(row(rbuf, k, s // 2, ch, pl.ds(s % 2, 1)), p_lo[f]), acc
                )
            if ch < 28:
                j, c = ch % 2, ch // 2
            else:
                j, c = 0, ch - 28 + COMPS
            return jnp.where(p_rem[f] == 8, take(row(cdiag, j, pl.ds(c, 1)), p_lo[f]), acc)

        for f in range(3):
            if k == 2:
                kept_ref[6 + f] = beyond(f, 29)
            outer_q = beyond(f, 28)
            half_speed = 0.5 * jnp.sqrt(1.0 + 0.03125 * (q[f] + outer_q))
            outer = [beyond(f, a) for a in range(8)]
            for a in range(8):
                r = (a // 2) * 3 + FACE_NODES[f][a % 2]
                total = half_speed * (edge[f] * tab[r] - outer[a])
                for b in range(8):
                    total = total - fout[b, a] * outer[b]
                pre[r] = pre[r] + total
            term = jnp.zeros(TILE, F32)
            for ch in range(8, 28):
                r = 12 + ((ch - 8) // 2) * 3 + FACE_NODES[f][ch % 2]
                value = beyond(f, ch)
                term = term + value * x[r]
                pre[r] = pre[r] + value
            far_terms[f] = far_terms[f] + weight * term

        for r in range(42):
            if k == 2:
                lam[1, r] = (2.0 / 3.0) * (cot[r] + DT * pre[r])
            elif k == 1:
                lam[0, r] = 0.25 * (lam[1, r] + DT * pre[r])
            else:
                out[r] = cot[r] * (1.0 / 3.0) + 0.75 * lam[1, r] + lam[0, r] + DT * pre[r]

    base = 4 * (ix * GY + iy)
    friction_bins = [jnp.zeros(TILE, F32) for _ in range(WINDOW // 8)]
    conduct_bins = [jnp.zeros(TILE, F32) for _ in range(WINDOW // 8)]
    own_rel = (zone - base + BEHIND + ZONES) & (ZONES - 1)
    far_rel = [(kept_ref[6 + f].astype(jnp.int32) - base + BEHIND + ZONES) & (ZONES - 1) for f in range(3)]
    for s in range(8):
        rel = jnp.broadcast_to(own_rel[s : s + 1], TILE) - sub
        tf_row = jnp.broadcast_to(tf[s : s + 1], TILE)
        tc_row = jnp.broadcast_to(tc[s : s + 1], TILE)
        for z in (4, 5):
            hit = rel == 8 * z
            friction_bins[z] = friction_bins[z] + jnp.where(hit, tf_row, 0.0)
            conduct_bins[z] = conduct_bins[z] + jnp.where(hit, tc_row, 0.0)
        for f in range(3):
            rel = jnp.broadcast_to(far_rel[f][s : s + 1], TILE) - sub
            term = jnp.broadcast_to(far_terms[f][s : s + 1], TILE)
            for z in range(WINDOW // 8):
                conduct_bins[z] = conduct_bins[z] + jnp.where(rel == 8 * z, term, 0.0)
    ones = jnp.ones(TILE, F32)
    pad = [jnp.zeros(TILE, F32) for _ in range(16 - WINDOW // 8)]

    def lanes(bins):
        return lax.dot_general(
            ones, jnp.concatenate(bins + pad, axis=0), (((1,), (1,)), ((), ())),
            precision=lax.Precision.HIGHEST, preferred_element_type=F32,
        )

    friction_row, conduct_row = lanes(friction_bins), lanes(conduct_bins)
    wide = (sub >> 1) * 128 + lane
    rel = (wide - base + BEHIND + ZONES) & (ZONES - 1)
    spread = jnp.where(
        (sub & 1) == 0, take(friction_row, rel & 127), take(conduct_row, rel & 127)
    )
    spread = jnp.where(rel < WINDOW, spread, 0.0)

    gyb[iy] = spread
    group = [
        pltpu.make_async_remote_copy(
            src_ref=gyb.at[iy], dst_ref=gyb.at[iy], send_sem=gy_send.at[d], recv_sem=gy_recv.at[d],
            device_id=at(0, d), device_id_type=MESH,
        )
        for d in range(1, GY)
    ]
    for copy in group:
        copy.start()
    started += group
    for copy in group:
        copy.wait_recv()
    total = gyb[0]
    for i in range(1, GY):
        total = total + gyb[i]
    gxb[ix] = total
    group = [
        pltpu.make_async_remote_copy(
            src_ref=gxb.at[ix], dst_ref=gxb.at[ix], send_sem=gx_send.at[d], recv_sem=gx_recv.at[d],
            device_id=at(d, 0), device_id_type=MESH,
        )
        for d in range(1, GX)
    ]
    for copy in group:
        copy.start()
    started += group
    for copy in group:
        copy.wait_recv()
    total = gxb[0]
    for i in range(1, GX):
        total = total + gxb[i]
    for t in range(4):
        grads[0:1, t * 128 : (t + 1) * 128] = GRAD_WEIGHT * total[2 * t : 2 * t + 1]
        grads[1:2, t * 128 : (t + 1) * 128] = (
            GRAD_WEIGHT * total[2 * t + 1 : 2 * t + 2] / zc_ref[t : t + 1]
        )
    for copy in started:
        copy.wait_send()


def local(
    cotangent, section_states, inverse_area, edge_length, roughness, soil_conductance, zone_friction,
    zone_conductivity, wet_mask, element_zone, send_face, send_count, face_partner, volume_matrix, flux_in, flux_out,
):
    vmem = pl.BlockSpec(memory_space=pltpu.VMEM)
    smem = pl.BlockSpec(memory_space=pltpu.SMEM)
    adjoint, grads = pl.pallas_call(
        kernel,
        out_shape=(
            jax.ShapeDtypeStruct((42, 8, 128), F32),
            jax.ShapeDtypeStruct((2, ZONES), F32),
        ),
        in_specs=[vmem] * 12 + [smem] * 3,
        out_specs=(vmem, vmem),
        scratch_shapes=[
            pltpu.VMEM((48, 8, 128), F32),
            pltpu.VMEM((48, 8, 128), F32),
            pltpu.VMEM((3, 42, 8, 128), F32),
            pltpu.VMEM((3, 30, 8, 128), F32),
            pltpu.VMEM((42, 8, 128), F32),
            pltpu.VMEM((2, 42, 8, 128), F32),
            pltpu.VMEM((9, 8, 128), F32),
            pltpu.VMEM((3, 4, 30, 2, 128), F32),
            pltpu.VMEM((3, 4, 30, 2, 128), F32),
            pltpu.VMEM((3, 2, 16, 128), F32),
            pltpu.VMEM((3, 4, 2, 16, 128), F32),
            pltpu.VMEM((2, 16, 128), F32),
            pltpu.VMEM((GY, 8, 128), F32),
            pltpu.VMEM((GX, 8, 128), F32),
            pltpu.SemaphoreType.DMA((3, 8)),
            pltpu.SemaphoreType.DMA((3, 8)),
            pltpu.SemaphoreType.DMA((GY,)),
            pltpu.SemaphoreType.DMA((GY,)),
            pltpu.SemaphoreType.DMA((GX,)),
            pltpu.SemaphoreType.DMA((GX,)),
        ],
        compiler_params=pltpu.CompilerParams(
            collective_id=0, has_side_effects=True, vmem_limit_bytes=32 << 20
        ),
        name="sections",
    )(
        cotangent.reshape(42, 8, 128),
        section_states.reshape(3, 42, 1024),
        inverse_area.reshape(8, 128),
        edge_length.reshape(3, 8, 128),
        roughness.reshape(8, 128),
        soil_conductance.reshape(8, 128),
        zone_friction.reshape(4, 128),
        zone_conductivity.reshape(4, 128),
        wet_mask.reshape(8, 128),
        element_zone.reshape(8, 128),
        send_face.reshape(8, 256),
        face_partner.reshape(3, 8, 128),
        volume_matrix,
        flux_in,
        flux_out,
    )
    return adjoint.reshape(1, 1, 42, 1024), grads


def solution(mesh):
    placed = (
        P("gx", "gy", None, None),
        P(None, "gx", "gy", None, None),
        P("gx", "gy", None),
        P("gx", "gy", None, None),
        P("gx", "gy", None),
        P("gx", "gy", None),
        P(),
        P(),
        P("gx", "gy", None),
        P("gx", "gy", None),
        P("gx", "gy", None, None),
        P("gx", "gy", None),
        P("gx", "gy", None, None),
        P(),
        P(),
        P(),
    )
    return jax.shard_map(
        local,
        mesh=mesh,
        in_specs=placed,
        out_specs=(P("gx", "gy", None, None), P()),
        check_vma=False,
    )
```

```python
import jax
import jax.numpy as jnp
from jax import lax
from jax.experimental import pallas as pl
from jax.experimental.pallas import tpu as pltpu
from jax.sharding import PartitionSpec as P

GX, GY = 16, 8
COMPS = 14
QCOMP, ZCOMP = 14, 15
ZONES = 512
DT = 0.2
GRAD_WEIGHT = 1.0 / 64.0
FACE_NODES = ((1, 2), (2, 0), (0, 1))
MAIN = (1, 3, 4, 6)
DIAG = (0, 2, 5, 7)
STEPS = ((-1, -1), (-1, 0), (-1, 1), (0, -1), (0, 1), (1, -1), (1, 0), (1, 1))
WINDOW, BEHIND = 80, 36
MESH = pl.DeviceIdType.MESH
TILE = (8, 128)
F32 = jnp.float32


LOOKUP = lax.GatherDimensionNumbers(
    offset_dims=(), collapsed_slice_dims=(1,), start_index_map=(1,), operand_batching_dims=(0,),
    start_indices_batching_dims=(0,),
)


def lanes_of(idx):
    return idx.reshape(8, 128, 1)


def take(x, idx):
    return lax.gather(
        x, idx, LOOKUP, slice_sizes=(1, 1), mode=lax.GatherScatterMode.PROMISE_IN_BOUNDS
    )


def row(ref, *at):
    return jnp.broadcast_to(ref[at], TILE)


def pick(code, values, like):
    out = jnp.full(TILE, values[-1], like.dtype)
    for i in range(len(values) - 2, -1, -1):
        out = jnp.where(code == i, values[i], out)
    return out


def ends(nodes, is0, is1):
    a, b, c = nodes
    first = lax.select(is0, b, lax.select(is1, c, a))
    second = lax.select(is0, c, lax.select(is1, a, b))
    return first, second


def kernel(
    cot_hbm, states_hbm, area_hbm, edge_hbm, rough_hbm, soil_hbm, zf_hbm, zc_hbm, wet_hbm, zone_hbm, send_hbm,
    partner_hbm, vol_hbm, fin_hbm, fout_hbm,
    out, grads,
    cot, states, area_ref, edge_ref, rough_ref, soil_ref, zf_ref, zc_ref, wet_ref, zone_ref, send_ref, partner_ref,
    vol_ref, fin_ref, fout_ref, vol, fin, fout,
    tab, aux, xs, local, fwd, pre, lam, kept, sbuf, rbuf, sdiag, rdiag, cdiag, gyb, gxb,
    in_sem, send_sem, recv_sem, gy_send, gy_recv, gx_send, gx_recv,
):
    ix, iy = lax.axis_index("gx"), lax.axis_index("gy")

    def at(dx, dy):
        return (lax.rem(ix + dx + GX, GX), lax.rem(iy + dy + GY, GY))

    side_x = {-1: (ix + GX - 1) // GX, 0: 1, 1: (2 * GX - 2 - ix) // GX}
    side_y = {-1: (iy + GY - 1) // GY, 0: 1, 1: (2 * GY - 2 - iy) // GY}

    def exists(n):
        dx, dy = STEPS[n]
        return side_x[dx] * side_y[dy] == 1

    barrier = pltpu.get_barrier_semaphore()
    peers = [at(0, k) for k in range(1, GY)] + [at(k, 0) for k in range(1, GX)]
    for n in DIAG:
        @pl.when(exists(n))
        def _():
            pl.semaphore_signal(barrier, inc=1, device_id=at(*STEPS[n]), device_id_type=MESH)
    for peer in reversed(peers):
        pl.semaphore_signal(barrier, inc=1, device_id=peer, device_id_type=MESH)
    greeters = len(peers) + (side_x[-1] + side_x[1]) * (side_y[-1] + side_y[1])

    inputs = (
        (cot_hbm, cot), (states_hbm, states), (area_hbm, area_ref), (edge_hbm, edge_ref), (rough_hbm, rough_ref),
        (soil_hbm, soil_ref), (zf_hbm, zf_ref), (zc_hbm, zc_ref), (wet_hbm, wet_ref), (zone_hbm, zone_ref),
        (send_hbm, send_ref), (partner_hbm, partner_ref), (vol_hbm, vol_ref), (fin_hbm, fin_ref), (fout_hbm, fout_ref),
    )
    reads = [pltpu.make_async_copy(src, dst, in_sem.at[i]) for i, (src, dst) in enumerate(inputs)]
    for read in reads:
        read.start()
    for read in reads:
        read.wait()

    sub = lax.broadcasted_iota(jnp.int32, TILE, 0)
    lane = lax.broadcasted_iota(jnp.int32, TILE, 1)

    area = area_ref[...]
    rough = rough_ref[...]
    wet = wet_ref[...].astype(F32)
    zone = zone_ref[...]
    edge = [edge_ref[f] for f in range(3)]
    kappa = jnp.zeros(TILE, F32)
    zfric = jnp.zeros(TILE, F32)
    zlane, zhi = lanes_of(zone & 127), zone >> 7
    for t in range(4):
        kappa = jnp.where(zhi == t, take(row(zc_ref, pl.ds(t, 1)), zlane), kappa)
        zfric = jnp.where(zhi == t, take(row(zf_ref, pl.ds(t, 1)), zlane), zfric)
    kappa = kappa * soil_ref[...]
    half_kappa = 0.5 * kappa
    rough_zone = zfric * rough

    slots = jnp.concatenate(
        [send_ref[n : n + 1, h * 128 : (h + 1) * 128] for n in MAIN for h in range(2)], axis=0
    )
    m_lo, m_f = lanes_of(slots & 127), slots >> 10
    m_hi = [((slots >> 7) & 7) == t for t in range(8)]
    m_is0, m_is1 = m_f == 0, m_f == 1
    dslots = jnp.zeros(TILE, jnp.int32)
    for i, n in enumerate(DIAG):
        first = jnp.broadcast_to(send_ref[n : n + 1, 0:128], TILE)
        d = 3 - i
        moved = pltpu.roll(first, 4 * d, axis=1) if d else first
        dslots = jnp.where((lane >> 2) == d, moved, dslots)
    d_lo, d_f = lanes_of(dslots & 127), dslots >> 10
    d_hi = [((dslots >> 7) & 7) == t for t in range(8)]
    d_is0, d_is1 = d_f == 0, d_f == 1

    p_lo, p_loc, p_rem, p_is0, p_is1 = [], [], [], [], []
    for f in range(3):
        p = partner_ref[f]
        there = p - 3072
        n = there >> 8
        slot_row = pick(n, (8, 0, 8, 2, 4, 8, 6, 8), p) + ((there >> 7) & 1)
        is_diag = (n == 0) | (n == 2) | (n == 5) | (n == 7)
        far = p >= 3072
        d_lane = pick(n, (0, 0, 4, 0, 0, 8, 0, 12), p) + (p & 3)
        p_lo.append(lanes_of(jnp.where(far & is_diag, d_lane, p & 127)))
        chunk = jnp.where(far, -1, (p >> 7) & 7)
        p_loc.append([chunk == t for t in range(8)])
        chunk = jnp.where(far, jnp.where(is_diag, 8, slot_row), -1)
        p_rem.append([chunk == t for t in range(9)])
        p_is0.append((p >> 10) == 0)
        p_is1.append((p >> 10) == 1)

    def from_slots(ref, c):
        nodes = []
        for n in range(3):
            acc = jnp.zeros(TILE, F32)
            for s in range(8):
                acc = lax.select(m_hi[s], take(row(ref, c * 3 + n, pl.ds(s, 1)), m_lo), acc)
            nodes.append(acc)
        return ends(nodes, m_is0, m_is1)

    def from_partner(ref, c, f):
        nodes = []
        for n in range(3):
            acc = jnp.zeros(TILE, F32)
            for s in range(8):
                acc = lax.select(p_loc[f][s], take(row(ref, c * 3 + n, pl.ds(s, 1)), p_lo[f]), acc)
            nodes.append(acc)
        return ends(nodes, p_is0[f], p_is1[f])

    def from_diag(ref, first, count):
        rows = ref.shape[0]
        flat = ref.reshape(rows * 8, 128)
        parts = []
        for h in range(count):
            nodes = []
            for n in range(3):
                acc = jnp.zeros(TILE, F32)
                for s in range(8):
                    got = flat[pl.ds(((first + h * 8) * 3 + n) * 8 + s, 8, stride=24), :]
                    acc = lax.select(d_hi[s], take(got, d_lo), acc)
                nodes.append(acc)
            parts.append(ends(nodes, d_is0, d_is1))
        return parts

    for small, wide, size in ((vol_ref, vol, 12), (fin_ref, fin, 8), (fout_ref, fout, 8)):
        for b in range(size):
            for a in range(size):
                wide[b * size + a] = jnp.broadcast_to(small[b : b + 1, a : a + 1], TILE)

    for f in range(3):
        aux[FACE_NODES[f][0]] = edge[f]
        aux[3 + f] = half_kappa
    for r in range(6, 24):
        aux[r] = jnp.zeros(TILE, F32)
    for r in range(45, 48):
        tab[r] = zone.astype(F32)
    slot_edge = from_slots(aux, 0)[0]
    slot_kedge = from_slots(aux, 1)[0] * slot_edge
    d_aux = from_diag(aux, 0, 1)[0][0]
    d_edge = jnp.broadcast_to(d_aux[0:1], TILE)
    d_kedge = jnp.broadcast_to(d_aux[1:2], TILE) * d_edge
    d_scale = [jnp.where(sub < 4, d_edge, d_kedge), jnp.where(sub < 6, d_kedge, 1.0)]
    kedge = [half_kappa * edge[f] for f in range(3)]

    sends = []

    def remote(src, dst, ssem, rsem, n):
        return pltpu.make_async_remote_copy(
            src_ref=src, dst_ref=dst, send_sem=ssem, recv_sem=rsem, device_id=at(*STEPS[n]), device_id_type=MESH
        )

    def main_copy(k, i):
        return remote(
            sbuf.at[k, i], rbuf.at[k, 3 - i], send_sem.at[k, i], recv_sem.at[k, 3 - i], MAIN[i]
        )

    def diag_copy(k, i):
        return remote(
            sdiag.at[k], rdiag.at[k, 3 - i], send_sem.at[k, 4 + i], recv_sem.at[k, 7 - i], DIAG[i]
        )

    def send(make, k, table, order):
        for i in order:
            @pl.when(exists(table[i]))
            def _():
                make(k, i).start()
            sends.append((make, k, table, i))

    def arrive(make, k, table, which):
        for i in which:
            @pl.when(exists(table[i]))
            def _():
                make(k, 3 - i).wait_recv()

    def send_slots(k, ref, comps, first_channel, scales):
        for c in comps:
            pair = from_slots(ref, c)
            for j in range(2 if c < COMPS else 1):
                value = pair[j] * scales(c) if c < COMPS and scales else pair[j]
                ch = c * 2 + j - first_channel if c < COMPS else 28 + c - COMPS
                for d in range(4):
                    sbuf[k, d, ch] = value[2 * d : 2 * d + 2]
        send(main_copy, k, MAIN, (0, 3, 1, 2))

    def merge_diag(k):
        for j in range(2):
            for h in range(2):
                acc = rdiag[k, 0, j, h * 8 : h * 8 + 8]
                for d in range(1, 4):
                    acc = jnp.where((lane >> 2) == d, rdiag[k, d, j, h * 8 : h * 8 + 8], acc)
                cdiag[k, j, h * 8 : h * 8 + 8] = acc

    def receive(k, ref, channels, rows):
        for f in range(3):
            for ch in channels:
                acc = ref[f, ch]
                for s in rows:
                    acc = lax.select(
                        p_rem[f][s], take(row(rbuf, k, s // 2, ch, pl.ds(s % 2, 1)), p_lo[f]), acc
                    )
                ref[f, ch] = acc

    def receive_diag(k, ref, f, ch, c, j):
        return lax.select(p_rem[f][8], take(row(cdiag, k, j, pl.ds(c, 1)), p_lo[f]), ref[f, ch])

    base = 4 * (ix * GY + iy)

    def relative(ids):
        return (ids - base + (BEHIND + ZONES)) & (ZONES - 1)

    tf = jnp.zeros(TILE, F32)
    tc = jnp.zeros(TILE, F32)
    far_terms = [jnp.zeros(TILE, F32)] * 3
    weights = {2: 2.0 / 3.0, 1: 0.25, 0: 1.0}
    FWD = 3

    def own_terms(k, v, x, weight, tf, tc):
        moment = jnp.sqrt(1.0 + (1.0 / 6.0) * sum(x[r] * x[r] for r in range(3, 9)))
        acc = jnp.zeros(TILE, F32)
        for r in range(3, 9):
            acc = acc + v[r] * x[r]
        tf = tf - weight * (wet * rough * moment) * acc
        flows = jnp.zeros(TILE, F32)
        faces = jnp.zeros(TILE, F32)
        for n in range(3):
            above = v[12 + n] - 0.5 * wet * v[9 + n]
            flows = flows + above * (x[9 + n] - x[12 + n])
            acc = tab[12 + n] * x[12 + n]
            for l in range(10):
                r = 12 + l * 3 + n
                if l:
                    acc = acc + tab[r] * x[r]
                if l < 9:
                    flows = flows + (v[r + 3] - v[r]) * (x[r] - x[r + 3])
            faces = faces + sum(kedge[f] for f in range(3) if n in FACE_NODES[f]) * acc
        tc = tc + weight * (kappa * flows - faces)
        return tf, tc, wet * rough_zone * moment

    def zone_bins(tf, tc):
        bins_f = [jnp.zeros(TILE, F32) for _ in range(WINDOW // 8)]
        bins_c = [jnp.zeros(TILE, F32) for _ in range(WINDOW // 8)]
        none = jnp.zeros(TILE, F32)
        own_rel = relative(zone)
        far_rel = [relative(kept[6 + f].astype(jnp.int32)) for f in range(3)]
        for s in range(8):
            rel = jnp.broadcast_to(own_rel[s : s + 1], TILE) - sub
            tf_row = jnp.broadcast_to(tf[s : s + 1], TILE)
            tc_row = jnp.broadcast_to(tc[s : s + 1], TILE)
            for z in (4, 5):
                hit = rel == 8 * z
                bins_f[z] = bins_f[z] + lax.select(hit, tf_row, none)
                bins_c[z] = bins_c[z] + lax.select(hit, tc_row, none)
            for f in range(3):
                rel = jnp.broadcast_to(far_rel[f][s : s + 1], TILE) - sub
                term = jnp.broadcast_to(far_terms[f][s : s + 1], TILE)
                for z in range(WINDOW // 8):
                    bins_c[z] = bins_c[z] + lax.select(rel == 8 * z, term, none)
        ones = jnp.ones(TILE, F32)
        pad = [jnp.zeros(TILE, F32) for _ in range(16 - WINDOW // 8)]

        def lanes(bins):
            return lax.dot_general(
                ones, jnp.concatenate(bins + pad, axis=0), (((1,), (1,)), ((), ())),
                precision=lax.Precision.HIGHEST, preferred_element_type=F32,
            )

        friction_row, conduct_row = lanes(bins_f), lanes(bins_c)
        rel = relative((sub >> 1) * 128 + lane)
        at_rel = lanes_of(rel & 127)
        spread = jnp.where(
            (sub & 1) == 0, take(friction_row, at_rel), take(conduct_row, at_rel)
        )
        return jnp.where(rel < WINDOW, spread, 0.0)

    gy_copies = [
        pltpu.make_async_remote_copy(
            src_ref=gyb.at[iy], dst_ref=gyb.at[iy], send_sem=gy_send.at[d], recv_sem=gy_recv.at[d],
            device_id=at(0, d), device_id_type=MESH,
        )
        for d in (4, 3, 5, 2, 6, 1, 7)
    ]
    gx_copies = [
        pltpu.make_async_remote_copy(
            src_ref=gxb.at[ix], dst_ref=gxb.at[ix], send_sem=gx_send.at[d], recv_sem=gx_recv.at[d],
            device_id=at(d, 0), device_id_type=MESH,
        )
        for d in (8, 6, 10, 7, 9, 5, 11, 4, 12, 3, 13, 2, 14, 1, 15)
    ]

    for k in (2, 1, 0):
        v = cot if k == 2 else lam.at[k]
        weight = weights[k] * DT
        x = xs.at[k]
        if k == 2:
            for m in (2, 0, 1):
                xflat = xs.at[m].reshape(42 * 8, 128)
                for s in range(8):
                    xflat[pl.ds(s, 42, stride=8), :] = states[m, :, s * 128 : (s + 1) * 128].astype(F32)
        squares = []
        for n in range(3):
            squares.append(sum(x[c * 3 + n] * x[c * 3 + n] for c in range(4)))
        q = [squares[a] + squares[b] for a, b in FACE_NODES]
        for f in range(3):
            tab[42 + FACE_NODES[f][0]] = q[f]
        wet_area = wet * area
        for r in range(12):
            tab[r] = wet_area * v[r]
        for r in range(12, 42):
            tab[r] = area * v[r]

        if k == 0:
            tf, tc, wet_friction = own_terms(k, v, x, weight, tf, tc)
            for f in range(3):
                term = jnp.zeros(TILE, F32)
                for ch in range(8, 28):
                    r = 12 + ((ch - 8) // 2) * 3 + FACE_NODES[f][ch % 2]
                    term = term + fwd[f, ch - 8] * tab[r]
                tc = tc + weight * kedge[f] * term
            gyb[iy] = zone_bins(tf, tc)
            for copy in gy_copies:
                copy.start()

        last = ZCOMP if k == 2 else QCOMP
        halves = from_diag(tab, 0, 2)
        for h in range(2):
            for j in range(2):
                sdiag[k, j, h * 8 : h * 8 + 8] = halves[h][j] * d_scale[h]
        if k == 2:
            pl.semaphore_wait(barrier, greeters)
        send(diag_copy, k, DIAG, (0, 1, 2, 3))
        send_slots(k, tab, range(last + 1), 0, lambda c: slot_edge if c < 4 else slot_kedge)

        if k == 2:
            for f in range(3):
                outer_edge = from_partner(aux, 0, f)[0]
                kept[f] = outer_edge
                kept[3 + f] = from_partner(aux, 1, f)[0] * outer_edge
        for f in range(3):
            for c in range(last + 1):
                pair = from_partner(tab, c, f)
                if c < COMPS:
                    scale = kept[f] if c < 4 else kept[3 + f]
                    local[f, c * 2] = pair[0] * scale
                    local[f, c * 2 + 1] = pair[1] * scale
                else:
                    local[f, 28 + c - COMPS] = pair[0]

        if k > 0:
            tf, tc, wet_friction = own_terms(k, v, x, weight, tf, tc)
        bars = [None] * 12
        for r in range(12):
            bars[r] = sum(vol[b * 12 + r] * tab[b] for b in range(12))
            if 3 <= r < 9:
                bars[r] = bars[r] - wet_friction * v[r]
        for f in range(3):
            for a in range(8):
                total = sum(
                    fin[b * 8 + a] * tab[(b // 2) * 3 + FACE_NODES[f][b % 2]] for b in range(8)
                )
                r = (a // 2) * 3 + FACE_NODES[f][a % 2]
                bars[r] = bars[r] + edge[f] * total
        for n in range(3):
            node_edge = sum(kedge[f] for f in range(3) if n in FACE_NODES[f])
            above = v[12 + n] - 0.5 * wet * v[9 + n]
            bars[9 + n] = bars[9 + n] + kappa * above
            for l in range(10):
                r = 12 + l * 3 + n
                below = v[r + 3] - v[r] if l < 9 else 0.0
                pre[r] = kappa * (below - above) - node_edge * tab[r]
                above = below
        for r in range(12):
            pre[r] = bars[r]

        if k == 2:
            halves = from_diag(xs.at[0], 4, 1) + from_diag(xs.at[0], 6, 1)
            for h in range(2):
                for j in range(2):
                    sdiag[FWD, j, h * 8 : h * 8 + 8] = halves[h][j]
            send(diag_copy, FWD, DIAG, (0, 1, 2, 3))
            send_slots(FWD, xs.at[0], range(4, COMPS), 8, None)
        if k == 1:
            for f in range(3):
                for c in range(4, COMPS):
                    pair = from_partner(xs.at[0], c, f)
                    fwd[f, c * 2 - 8] = pair[0]
                    fwd[f, c * 2 - 7] = pair[1]
            arrive(main_copy, FWD, MAIN, range(4))
            arrive(diag_copy, FWD, DIAG, range(4))
            merge_diag(FWD)
            receive(FWD, fwd, range(20), range(8))
            for f in range(3):
                for ch in range(20):
                    c = ch // 2 if ch < 4 else ch // 2 + 6
                    fwd[f, ch] = receive_diag(FWD, fwd, f, ch, c, ch % 2)
        if k == 0:
            for copy in gy_copies:
                copy.wait_recv()
            total = gyb[0]
            for i in range(1, GY):
                total = total + gyb[i]
            gxb[ix] = total
            for copy in gx_copies:
                copy.start()

        channels = range(30 if k == 2 else 29)
        arrive(main_copy, k, MAIN, (1, 2))
        receive(k, local, channels, range(2, 6))
        arrive(main_copy, k, MAIN, (0, 3))
        receive(k, local, channels, (0, 1, 6, 7))
        arrive(diag_copy, k, DIAG, range(4))
        merge_diag(k)
        for f in range(3):
            if k == 2:
                kept[6 + f] = receive_diag(k, local, f, 29, ZCOMP, 0)
            outer_q = receive_diag(k, local, f, 28, QCOMP, 0)
            half_speed = 0.5 * jnp.sqrt(1.0 + 0.03125 * (q[f] + outer_q))
            outer = [receive_diag(k, local, f, a, a // 2, a % 2) for a in range(8)]
            for a in range(8):
                r = (a // 2) * 3 + FACE_NODES[f][a % 2]
                total = half_speed * (edge[f] * tab[r] - outer[a])
                for b in range(8):
                    total = total - fout[b * 8 + a] * outer[b]
                pre[r] = pre[r] + total
            term = jnp.zeros(TILE, F32)
            for ch in range(8, 28):
                r = 12 + ((ch - 8) // 2) * 3 + FACE_NODES[f][ch % 2]
                value = receive_diag(k, local, f, ch, ch // 2, ch % 2)
                if k > 0:
                    term = term + value * x[r]
                pre[r] = pre[r] + value
            far_terms[f] = far_terms[f] + weight * term

        for r in range(42):
            if k == 2:
                lam[1, r] = (2.0 / 3.0) * (cot[r] + DT * pre[r])
            elif k == 1:
                lam[0, r] = 0.25 * (lam[1, r] + DT * pre[r])
            else:
                out[r] = cot[r] * (1.0 / 3.0) + 0.75 * lam[1, r] + lam[0, r] + DT * pre[r]

    for copy in gx_copies:
        copy.wait_recv()
    total = gxb[0]
    for i in range(1, GX):
        total = total + gxb[i]
    for t in range(4):
        grads[0:1, t * 128 : (t + 1) * 128] = GRAD_WEIGHT * total[2 * t : 2 * t + 1]
        grads[1:2, t * 128 : (t + 1) * 128] = (
            GRAD_WEIGHT * total[2 * t + 1 : 2 * t + 2] / zc_ref[t : t + 1]
        )
    for make, k, table, i in sends:
        @pl.when(exists(table[i]))
        def _():
            make(k, i).wait_send()
    for copy in gy_copies + gx_copies:
        copy.wait_send()


def local(
    cotangent, section_states, inverse_area, edge_length, roughness, soil_conductance, zone_friction,
    zone_conductivity, wet_mask, element_zone, send_face, send_count, face_partner, volume_matrix, flux_in, flux_out,
):
    vmem = pl.BlockSpec(memory_space=pltpu.VMEM)
    adjoint, grads = pl.pallas_call(
        kernel,
        out_shape=(
            jax.ShapeDtypeStruct((42, 8, 128), F32),
            jax.ShapeDtypeStruct((2, ZONES), F32),
        ),
        in_specs=[pl.BlockSpec(memory_space=pl.ANY)] * 15,
        out_specs=(vmem, vmem),
        scratch_shapes=[
            pltpu.VMEM((42, 8, 128), F32),
            pltpu.VMEM((3, 42, 1024), jnp.bfloat16),
            pltpu.VMEM((8, 128), F32),
            pltpu.VMEM((3, 8, 128), F32),
            pltpu.VMEM((8, 128), F32),
            pltpu.VMEM((8, 128), F32),
            pltpu.VMEM((4, 128), F32),
            pltpu.VMEM((4, 128), F32),
            pltpu.VMEM((8, 128), jnp.int32),
            pltpu.VMEM((8, 128), jnp.int32),
            pltpu.VMEM((8, 256), jnp.int32),
            pltpu.VMEM((3, 8, 128), jnp.int32),
            pltpu.VMEM((12, 12), F32),
            pltpu.VMEM((8, 8), F32),
            pltpu.VMEM((8, 8), F32),
            pltpu.VMEM((144, 8, 128), F32),
            pltpu.VMEM((64, 8, 128), F32),
            pltpu.VMEM((64, 8, 128), F32),
            pltpu.VMEM((48, 8, 128), F32),
            pltpu.VMEM((24, 8, 128), F32),
            pltpu.VMEM((3, 42, 8, 128), F32),
            pltpu.VMEM((3, 30, 8, 128), F32),
            pltpu.VMEM((3, 20, 8, 128), F32),
            pltpu.VMEM((42, 8, 128), F32),
            pltpu.VMEM((2, 42, 8, 128), F32),
            pltpu.VMEM((9, 8, 128), F32),
            pltpu.VMEM((4, 4, 30, 2, 128), F32),
            pltpu.VMEM((4, 4, 30, 2, 128), F32),
            pltpu.VMEM((4, 2, 16, 128), F32),
            pltpu.VMEM((4, 4, 2, 16, 128), F32),
            pltpu.VMEM((4, 2, 16, 128), F32),
            pltpu.VMEM((GY, 8, 128), F32),
            pltpu.VMEM((GX, 8, 128), F32),
            pltpu.SemaphoreType.DMA((15,)),
            pltpu.SemaphoreType.DMA((4, 8)),
            pltpu.SemaphoreType.DMA((4, 8)),
            pltpu.SemaphoreType.DMA((GY,)),
            pltpu.SemaphoreType.DMA((GY,)),
            pltpu.SemaphoreType.DMA((GX,)),
            pltpu.SemaphoreType.DMA((GX,)),
        ],
        compiler_params=pltpu.CompilerParams(
            collective_id=0, has_side_effects=True, vmem_limit_bytes=63 << 20
        ),
        name="sections",
    )(
        cotangent.reshape(42, 8, 128),
        section_states.reshape(3, 42, 1024),
        inverse_area.reshape(8, 128),
        edge_length.reshape(3, 8, 128),
        roughness.reshape(8, 128),
        soil_conductance.reshape(8, 128),
        zone_friction.reshape(4, 128),
        zone_conductivity.reshape(4, 128),
        wet_mask.reshape(8, 128),
        element_zone.reshape(8, 128),
        send_face.reshape(8, 256),
        face_partner.reshape(3, 8, 128),
        volume_matrix,
        flux_in,
        flux_out,
    )
    return adjoint.reshape(1, 1, 42, 1024), grads


def solution(mesh):
    placed = (
        P("gx", "gy", None, None),
        P(None, "gx", "gy", None, None),
        P("gx", "gy", None),
        P("gx", "gy", None, None),
        P("gx", "gy", None),
        P("gx", "gy", None),
        P(),
        P(),
        P("gx", "gy", None),
        P("gx", "gy", None),
        P("gx", "gy", None, None),
        P("gx", "gy", None),
        P("gx", "gy", None, None),
        P(),
        P(),
        P(),
    )
    return jax.shard_map(
        local,
        mesh=mesh,
        in_specs=placed,
        out_specs=(P("gx", "gy", None, None), P()),
        check_vma=False,
    )
```

```python
import jax
import jax.numpy as jnp
from jax import lax
from jax.experimental import pallas as pl
from jax.experimental.pallas import tpu as pltpu
from jax.sharding import PartitionSpec as P

GX, GY = 16, 8
COMPS = 14
QCOMP, ZCOMP = 14, 15
ZONES = 512
DT = 0.2
GRAD_WEIGHT = 1.0 / 64.0
SPLIT = 7
FIRST = 2 + 2 * SPLIT
FACE_NODES = ((1, 2), (2, 0), (0, 1))
MAIN = (1, 3, 4, 6)
DIAG = (0, 2, 5, 7)
STEPS = ((-1, -1), (-1, 0), (-1, 1), (0, -1), (0, 1), (1, -1), (1, 0), (1, 1))
WINDOW, BEHIND = 88, 40
MESH = pl.DeviceIdType.MESH
TILE = (8, 128)
F32 = jnp.float32


LOOKUP = lax.GatherDimensionNumbers(
    offset_dims=(), collapsed_slice_dims=(1,), start_index_map=(1,), operand_batching_dims=(0,),
    start_indices_batching_dims=(0,),
)


def lanes_of(idx):
    return idx.reshape(8, 128, 1)


def take(x, idx):
    return lax.gather(
        x, idx, LOOKUP, slice_sizes=(1, 1), mode=lax.GatherScatterMode.PROMISE_IN_BOUNDS
    )


def row(ref, *at):
    return jnp.broadcast_to(ref[at], TILE)


def pick(code, values, like):
    out = jnp.full(TILE, values[-1], like.dtype)
    for i in range(len(values) - 2, -1, -1):
        out = jnp.where(code == i, values[i], out)
    return out


def ends(nodes, is0, is1):
    a, b, c = nodes
    first = lax.select(is0, b, lax.select(is1, c, a))
    second = lax.select(is0, c, lax.select(is1, a, b))
    return first, second


def kernel(
    cot_hbm, states_hbm, area_hbm, edge_hbm, rough_hbm, soil_hbm, zf_hbm, zc_hbm, wet_hbm, zone_hbm, send_hbm,
    partner_hbm, vol_hbm, fin_hbm, fout_hbm,
    out, grads,
    cot, states, area_ref, edge_ref, rough_ref, soil_ref, zf_ref, zc_ref, wet_ref, zone_ref, send_ref, partner_ref,
    vol_ref, fin_ref, fout_ref, vol, fin, fout,
    tab, aux, xs, local, fwd, pre, lam, kept, sbuf, rbuf, sdiag, rdiag, cdiag, gyb, gxb,
    in_sem, send_sem, recv_sem, gy_send, gy_recv, gx_send, gx_recv,
):
    ix, iy = lax.axis_index("gx"), lax.axis_index("gy")

    def at(dx, dy):
        return (lax.rem(ix + dx + GX, GX), lax.rem(iy + dy + GY, GY))

    side_x = {-1: (ix + GX - 1) // GX, 0: 1, 1: (2 * GX - 2 - ix) // GX}
    side_y = {-1: (iy + GY - 1) // GY, 0: 1, 1: (2 * GY - 2 - iy) // GY}

    def exists(n):
        dx, dy = STEPS[n]
        return side_x[dx] * side_y[dy] == 1

    barrier = pltpu.get_barrier_semaphore()
    peers = [at(k, 0) for k in (1, 15)] + [at(0, k) for k in (1, 7)]
    peers += [at(k, 0) for k in (8, 7, 9, 6, 10, 5, 11, 4, 12, 3, 13, 2, 14)]
    peers += [at(0, k) for k in (4, 3, 5, 2, 6)]
    for n in DIAG:
        @pl.when(exists(n))
        def _():
            pl.semaphore_signal(barrier, inc=1, device_id=at(*STEPS[n]), device_id_type=MESH)
    for peer in peers:
        pl.semaphore_signal(barrier, inc=1, device_id=peer, device_id_type=MESH)
    greeters = len(peers) + (side_x[-1] + side_x[1]) * (side_y[-1] + side_y[1])

    inputs = (
        (cot_hbm, cot), (states_hbm, states), (area_hbm, area_ref), (edge_hbm, edge_ref), (rough_hbm, rough_ref),
        (soil_hbm, soil_ref), (zf_hbm, zf_ref), (zc_hbm, zc_ref), (wet_hbm, wet_ref), (zone_hbm, zone_ref),
        (send_hbm, send_ref), (partner_hbm, partner_ref), (vol_hbm, vol_ref), (fin_hbm, fin_ref), (fout_hbm, fout_ref),
    )
    reads = [pltpu.make_async_copy(src, dst, in_sem.at[i]) for i, (src, dst) in enumerate(inputs)]
    for read in reads:
        read.start()
    for read in reads:
        read.wait()

    sub = lax.broadcasted_iota(jnp.int32, TILE, 0)
    lane = lax.broadcasted_iota(jnp.int32, TILE, 1)

    lane16 = [(lane >> 4) == g for g in range(4)]
    lane4 = [((lane >> 2) & 3) == d for d in range(4)]
    area = area_ref[...]
    rough = rough_ref[...]
    wet = wet_ref[...].astype(F32)
    zone = zone_ref[...]
    edge = [edge_ref[f] for f in range(3)]
    kappa = jnp.zeros(TILE, F32)
    zfric = jnp.zeros(TILE, F32)
    zlane, zhi = lanes_of(zone & 127), zone >> 7
    for t in range(4):
        kappa = jnp.where(zhi == t, take(row(zc_ref, pl.ds(t, 1)), zlane), kappa)
        zfric = jnp.where(zhi == t, take(row(zf_ref, pl.ds(t, 1)), zlane), zfric)
    kappa = kappa * soil_ref[...]
    half_kappa = 0.5 * kappa
    rough_zone = zfric * rough

    slots = jnp.concatenate(
        [send_ref[n : n + 1, h * 128 : (h + 1) * 128] for n in MAIN for h in range(2)], axis=0
    )
    m_lo, m_f = lanes_of(slots & 127), slots >> 10
    m_hi = [((slots >> 7) & 7) == t for t in range(8)]
    m_is0, m_is1 = m_f == 0, m_f == 1
    dslots = jnp.zeros(TILE, jnp.int32)
    for i, n in enumerate(DIAG):
        first = jnp.broadcast_to(send_ref[n : n + 1, 0:128], TILE)
        d = 3 - i
        moved = pltpu.roll(first, 4 * d, axis=1) if d else first
        dslots = jnp.where((lane >> 2) == d, moved, dslots)
    d_lo, d_f = lanes_of(dslots & 127), dslots >> 10
    d_hi = [((dslots >> 7) & 7) == t for t in range(8)]
    d_is0, d_is1 = d_f == 0, d_f == 1

    p_lo, p_loc, p_rem, p_is0, p_is1 = [], [], [], [], []
    for f in range(3):
        p = partner_ref[f]
        there = p - 3072
        n = there >> 8
        slot_row = pick(n, (8, 0, 8, 2, 4, 8, 6, 8), p) + ((there >> 7) & 1)
        is_diag = (n == 0) | (n == 2) | (n == 5) | (n == 7)
        far = p >= 3072
        d_lane = pick(n, (0, 0, 4, 0, 0, 8, 0, 12), p) + (p & 3)
        p_lo.append(lanes_of(jnp.where(far & is_diag, d_lane, p & 127)))
        chunk = jnp.where(far, -1, (p >> 7) & 7)
        p_loc.append([chunk == t for t in range(8)])
        chunk = jnp.where(far, jnp.where(is_diag, 8, slot_row), -1)
        p_rem.append([chunk == t for t in range(9)])
        p_is0.append((p >> 10) == 0)
        p_is1.append((p >> 10) == 1)

    def from_slots(ref, c):
        nodes = []
        for n in range(3):
            acc = jnp.zeros(TILE, F32)
            for s in range(8):
                acc = lax.select(m_hi[s], take(row(ref, c * 3 + n, pl.ds(s, 1)), m_lo), acc)
            nodes.append(acc)
        return ends(nodes, m_is0, m_is1)

    def from_partner(ref, c, f):
        nodes = []
        for n in range(3):
            acc = jnp.zeros(TILE, F32)
            for s in range(8):
                acc = lax.select(p_loc[f][s], take(row(ref, c * 3 + n, pl.ds(s, 1)), p_lo[f]), acc)
            nodes.append(acc)
        return ends(nodes, p_is0[f], p_is1[f])

    def from_diag(ref, first, count):
        rows = ref.shape[0]
        flat = ref.reshape(rows * 8, 128)
        parts = []
        for h in range(count):
            nodes = []
            for n in range(3):
                acc = jnp.zeros(TILE, F32)
                for s in range(8):
                    got = flat[pl.ds(((first + h * 8) * 3 + n) * 8 + s, 8, stride=24), :]
                    acc = lax.select(d_hi[s], take(got, d_lo), acc)
                nodes.append(acc)
            parts.append(ends(nodes, d_is0, d_is1))
        return parts

    for f in range(3):
        aux[FACE_NODES[f][0]] = edge[f]
        aux[3 + f] = half_kappa
    for r in range(6, 24):
        aux[r] = jnp.zeros(TILE, F32)
    for r in range(45, 48):
        tab[r] = zone.astype(F32)
    slot_edge = from_slots(aux, 0)[0]
    slot_kedge = from_slots(aux, 1)[0] * slot_edge
    d_aux = from_diag(aux, 0, 1)[0][0]
    d_edge = jnp.broadcast_to(d_aux[0:1], TILE)
    d_kedge = jnp.broadcast_to(d_aux[1:2], TILE) * d_edge
    d_scale = [jnp.where(sub < 4, d_edge, d_kedge), jnp.where(sub < 6, d_kedge, 1.0)]
    kedge = [half_kappa * edge[f] for f in range(3)]

    sends = []

    def remote(src, dst, ssem, rsem, n):
        return pltpu.make_async_remote_copy(
            src_ref=src, dst_ref=dst, send_sem=ssem, recv_sem=rsem, device_id=at(*STEPS[n]), device_id_type=MESH
        )

    def part_copy(k, i, rows, a):
        return remote(
            sbuf.at[k, i, rows], rbuf.at[k, 3 - i, rows], send_sem.at[k, a + i], recv_sem.at[k, a + 3 - i], MAIN[i]
        )

    def first_copy(k, i):
        return part_copy(k, i, pl.ds(0, FIRST), 0)

    def second_copy(k, i):
        return part_copy(k, i, pl.ds(FIRST, 30 - FIRST), 8)

    def forward_copy(k, i):
        return part_copy(k, i, pl.ds(0, 20), 0)

    def diag_copy(k, i):
        return remote(
            sdiag.at[k], rdiag.at[k, 3 - i], send_sem.at[k, 4 + i], recv_sem.at[k, 7 - i], DIAG[i]
        )

    def send(make, k, table, order):
        for i in order:
            @pl.when(exists(table[i]))
            def _():
                make(k, i).start()
            sends.append((make, k, table, i))

    def arrive(make, k, table, which):
        for i in which:
            @pl.when(exists(table[i]))
            def _():
                make(k, 3 - i).wait_recv()

    def fill_slots(k, ref, comps, first_channel, scales):
        for c in comps:
            pair = from_slots(ref, c)
            for j in range(2 if c < COMPS else 1):
                value = pair[j] * scales(c) if c < COMPS and scales else pair[j]
                ch = c * 2 + j + first_channel if c < COMPS else c - COMPS
                for d in range(4):
                    sbuf[k, d, ch] = value[2 * d : 2 * d + 2]

    def unpack_state(m):
        flat = xs.at[m].reshape(42 * 8, 128)
        for s in range(8):
            flat[pl.ds(s, 42, stride=8), :] = states[m, :, s * 128 : (s + 1) * 128].astype(F32)

    def pack_diag(k, halves, scales):
        packed = jnp.zeros(TILE, F32)
        for j in range(2):
            for h in range(2):
                g = 2 * j + h
                value = halves[h][j] * scales[h] if scales else halves[h][j]
                packed = lax.select(lane16[g], pltpu.roll(value, 16 * g, axis=1) if g else value, packed)
        sdiag[k] = packed
        send(diag_copy, k, DIAG, (0, 1, 2, 3))

    def merge_diag(k):
        acc = rdiag[k, 0]
        for d in range(1, 4):
            acc = lax.select(lane4[d], rdiag[k, d], acc)
        for j in range(2):
            for h in range(2):
                g = 2 * j + h
                cdiag[k, j, h * 8 : h * 8 + 8] = pltpu.roll(acc, 128 - 16 * g, axis=1) if g else acc

    def receive(k, ref, channels, rows):
        for f in range(3):
            for ch in channels:
                acc = ref[f, ch]
                for s in rows:
                    acc = lax.select(
                        p_rem[f][s], take(row(rbuf, k, s // 2, ch, pl.ds(s % 2, 1)), p_lo[f]), acc
                    )
                ref[f, ch] = acc

    def receive_diag(k, ref, f, ch, c, j):
        return lax.select(p_rem[f][8], take(row(cdiag, k, j, pl.ds(c, 1)), p_lo[f]), ref[f, ch])

    base = 4 * (ix * GY + iy)

    def relative(ids):
        return (ids - base + (BEHIND + ZONES)) & (ZONES - 1)

    tf = jnp.zeros(TILE, F32)
    tc = jnp.zeros(TILE, F32)
    far_terms = [jnp.zeros(TILE, F32)] * 3
    weights = {2: 2.0 / 3.0, 1: 0.25, 0: 1.0}
    FWD = 3

    def own_terms(k, v, x, weight, tf, tc):
        moment = jnp.sqrt(1.0 + (1.0 / 6.0) * sum(x[r] * x[r] for r in range(3, 9)))
        acc = jnp.zeros(TILE, F32)
        for r in range(3, 9):
            acc = acc + v[r] * x[r]
        tf = tf - weight * (wet * rough * moment) * acc
        flows = jnp.zeros(TILE, F32)
        faces = jnp.zeros(TILE, F32)
        for n in range(3):
            above = v[12 + n] - 0.5 * wet * v[9 + n]
            flows = flows + above * (x[9 + n] - x[12 + n])
            acc = tab[12 + n] * x[12 + n]
            for l in range(10):
                r = 12 + l * 3 + n
                if l:
                    acc = acc + tab[r] * x[r]
                if l < 9:
                    flows = flows + (v[r + 3] - v[r]) * (x[r] - x[r + 3])
            faces = faces + sum(kedge[f] for f in range(3) if n in FACE_NODES[f]) * acc
        tc = tc + weight * (kappa * flows - faces)
        return tf, tc, wet * rough_zone * moment

    def zone_bins(tf, tc):
        bins_f = [jnp.zeros(TILE, F32) for _ in range(WINDOW // 8)]
        bins_c = [jnp.zeros(TILE, F32) for _ in range(WINDOW // 8)]
        none = jnp.zeros(TILE, F32)
        own_rel = relative(zone)
        far_rel = [relative(kept[6 + f].astype(jnp.int32)) for f in range(3)]
        for s in range(8):
            rel = jnp.broadcast_to(own_rel[s : s + 1], TILE) - sub
            tf_row = jnp.broadcast_to(tf[s : s + 1], TILE)
            tc_row = jnp.broadcast_to(tc[s : s + 1], TILE)
            for z in (5,):
                hit = rel == 8 * z
                bins_f[z] = bins_f[z] + lax.select(hit, tf_row, none)
                bins_c[z] = bins_c[z] + lax.select(hit, tc_row, none)
            for f in range(3):
                rel = jnp.broadcast_to(far_rel[f][s : s + 1], TILE) - sub
                term = jnp.broadcast_to(far_terms[f][s : s + 1], TILE)
                for z in range(WINDOW // 8):
                    bins_c[z] = bins_c[z] + lax.select(rel == 8 * z, term, none)
        ones = jnp.ones(TILE, F32)
        pad = [jnp.zeros(TILE, F32) for _ in range(16 - WINDOW // 8)]

        def lanes(bins):
            return lax.dot_general(
                ones, jnp.concatenate(bins + pad, axis=0), (((1,), (1,)), ((), ())),
                precision=lax.Precision.HIGHEST, preferred_element_type=F32,
            )

        friction_row, conduct_row = lanes(bins_f), lanes(bins_c)
        rel = relative((sub >> 1) * 128 + lane)
        at_rel = lanes_of(rel & 127)
        spread = jnp.where(
            (sub & 1) == 0, take(friction_row, at_rel), take(conduct_row, at_rel)
        )
        return jnp.where(rel < WINDOW, spread, 0.0)

    gy_copies = [
        pltpu.make_async_remote_copy(
            src_ref=gyb.at[iy], dst_ref=gyb.at[iy], send_sem=gy_send.at[d], recv_sem=gy_recv.at[d],
            device_id=at(0, d), device_id_type=MESH,
        )
        for d in (4, 3, 5, 2, 6, 1, 7)
    ]
    gx_copies = [
        pltpu.make_async_remote_copy(
            src_ref=gxb.at[ix], dst_ref=gxb.at[ix], send_sem=gx_send.at[d], recv_sem=gx_recv.at[d],
            device_id=at(d, 0), device_id_type=MESH,
        )
        for d in (8, 6, 10, 7, 9, 5, 11, 4, 12, 3, 13, 2, 14, 1, 15)
    ]

    for k in (2, 1, 0):
        v = cot if k == 2 else lam.at[k]
        weight = weights[k] * DT
        x = xs.at[k]
        if k == 2:
            unpack_state(2)
        squares = []
        for n in range(3):
            squares.append(sum(x[c * 3 + n] * x[c * 3 + n] for c in range(4)))
        q = [squares[a] + squares[b] for a, b in FACE_NODES]
        for f in range(3):
            tab[42 + FACE_NODES[f][0]] = q[f]
        wet_area = wet * area
        for r in range(12):
            tab[r] = wet_area * v[r]
        for r in range(12, 42):
            tab[r] = area * v[r]

        if k == 0:
            tf, tc, wet_friction = own_terms(k, v, x, weight, tf, tc)
            for f in range(3):
                term = jnp.zeros(TILE, F32)
                for ch in range(8, 28):
                    r = 12 + ((ch - 8) // 2) * 3 + FACE_NODES[f][ch % 2]
                    term = term + fwd[f, ch - 8] * tab[r]
                tc = tc + weight * kedge[f] * term
            gyb[iy] = zone_bins(tf, tc)
            for copy in gy_copies:
                copy.start()

        last = ZCOMP if k == 2 else QCOMP
        if k < 2:
            pack_diag(k, from_diag(tab, 0, 2), d_scale)
        slot_scale = lambda c: slot_edge if c < 4 else slot_kedge
        fill_slots(k, tab, list(range(COMPS, last + 1)) + list(range(SPLIT)), 2, slot_scale)
        if k == 2:
            halves = from_diag(tab, 0, 2)
            pl.semaphore_wait(barrier, greeters)
            pack_diag(k, halves, d_scale)
        send(first_copy, k, MAIN, (0, 3, 1, 2))
        fill_slots(k, tab, range(SPLIT, COMPS), 2, slot_scale)
        send(second_copy, k, MAIN, (0, 3, 1, 2))

        if k == 2:
            for m in (0, 1):
                unpack_state(m)
            for small, wide, size in ((vol_ref, vol, 12), (fin_ref, fin, 8), (fout_ref, fout, 8)):
                for b in range(size):
                    for a in range(size):
                        wide[b * size + a] = jnp.broadcast_to(small[b : b + 1, a : a + 1], TILE)

        if k == 2:
            for f in range(3):
                outer_edge = from_partner(aux, 0, f)[0]
                kept[f] = outer_edge
                kept[3 + f] = from_partner(aux, 1, f)[0] * outer_edge
        for f in range(3):
            for c in range(last + 1):
                pair = from_partner(tab, c, f)
                if c < COMPS:
                    scale = kept[f] if c < 4 else kept[3 + f]
                    local[f, c * 2 + 2] = pair[0] * scale
                    local[f, c * 2 + 3] = pair[1] * scale
                else:
                    local[f, c - COMPS] = pair[0]

        if k > 0:
            tf, tc, wet_friction = own_terms(k, v, x, weight, tf, tc)
        bars = [None] * 12
        for r in range(12):
            bars[r] = sum(vol[b * 12 + r] * tab[b] for b in range(12))
            if 3 <= r < 9:
                bars[r] = bars[r] - wet_friction * v[r]
        for f in range(3):
            for a in range(8):
                total = sum(
                    fin[b * 8 + a] * tab[(b // 2) * 3 + FACE_NODES[f][b % 2]] for b in range(8)
                )
                r = (a // 2) * 3 + FACE_NODES[f][a % 2]
                bars[r] = bars[r] + edge[f] * total
        for n in range(3):
            node_edge = sum(kedge[f] for f in range(3) if n in FACE_NODES[f])
            above = v[12 + n] - 0.5 * wet * v[9 + n]
            bars[9 + n] = bars[9 + n] + kappa * above
            for l in range(10):
                r = 12 + l * 3 + n
                below = v[r + 3] - v[r] if l < 9 else 0.0
                pre[r] = kappa * (below - above) - node_edge * tab[r]
                above = below
        for r in range(12):
            pre[r] = bars[r]

        if k == 2:
            halves = from_diag(xs.at[0], 4, 1) + from_diag(xs.at[0], 6, 1)
            pack_diag(FWD, halves, None)
            fill_slots(FWD, xs.at[0], range(4, COMPS), -8, None)
            send(forward_copy, FWD, MAIN, (0, 3, 1, 2))
        if k == 1:
            for f in range(3):
                for c in range(4, COMPS):
                    pair = from_partner(xs.at[0], c, f)
                    fwd[f, c * 2 - 8] = pair[0]
                    fwd[f, c * 2 - 7] = pair[1]
            arrive(forward_copy, FWD, MAIN, range(4))
            arrive(diag_copy, FWD, DIAG, range(4))
            merge_diag(FWD)
            receive(FWD, fwd, range(20), range(8))
            for f in range(3):
                for ch in range(20):
                    c = ch // 2 if ch < 4 else ch // 2 + 6
                    fwd[f, ch] = receive_diag(FWD, fwd, f, ch, c, ch % 2)
        if k == 0:
            for copy in gy_copies:
                copy.wait_recv()
            total = gyb[0]
            for i in range(1, GY):
                total = total + gyb[i]
            gxb[ix] = total
            for copy in gx_copies:
                copy.start()

        early = [ch for ch in range(FIRST) if ch != 1 or k == 2]
        late = range(FIRST, 30)
        terms = [jnp.zeros(TILE, F32)] * 3

        def porewater(f, channels):
            for ch in channels:
                r = 12 + ((ch - 10) // 2) * 3 + FACE_NODES[f][ch % 2]
                value = receive_diag(k, local, f, ch, ch // 2 - 1, ch % 2)
                if k > 0:
                    terms[f] = terms[f] + value * x[r]
                pre[r] = pre[r] + value

        arrive(first_copy, k, MAIN, (1, 2))
        receive(k, local, early, range(2, 6))
        arrive(second_copy, k, MAIN, (1, 2))
        receive(k, local, late, range(2, 6))
        arrive(first_copy, k, MAIN, (0, 3))
        receive(k, local, early, (0, 1, 6, 7))
        arrive(diag_copy, k, DIAG, range(4))
        merge_diag(k)
        for f in range(3):
            if k == 2:
                kept[6 + f] = receive_diag(k, local, f, 1, ZCOMP, 0)
            outer_q = receive_diag(k, local, f, 0, QCOMP, 0)
            half_speed = 0.5 * jnp.sqrt(1.0 + 0.03125 * (q[f] + outer_q))
            outer = [receive_diag(k, local, f, a + 2, a // 2, a % 2) for a in range(8)]
            for a in range(8):
                r = (a // 2) * 3 + FACE_NODES[f][a % 2]
                total = half_speed * (edge[f] * tab[r] - outer[a])
                for b in range(8):
                    total = total - fout[b * 8 + a] * outer[b]
                pre[r] = pre[r] + total
            porewater(f, range(10, FIRST))
        arrive(second_copy, k, MAIN, (0, 3))
        receive(k, local, late, (0, 1, 6, 7))
        for f in range(3):
            porewater(f, late)
            far_terms[f] = far_terms[f] + weight * terms[f]

        for r in range(42):
            if k == 2:
                lam[1, r] = (2.0 / 3.0) * (cot[r] + DT * pre[r])
            elif k == 1:
                lam[0, r] = 0.25 * (lam[1, r] + DT * pre[r])
            else:
                out[r] = cot[r] * (1.0 / 3.0) + 0.75 * lam[1, r] + lam[0, r] + DT * pre[r]

    for copy in gx_copies:
        copy.wait_recv()
    total = gxb[0]
    for i in range(1, GX):
        total = total + gxb[i]
    for t in range(4):
        grads[0:1, t * 128 : (t + 1) * 128] = GRAD_WEIGHT * total[2 * t : 2 * t + 1]
        grads[1:2, t * 128 : (t + 1) * 128] = (
            GRAD_WEIGHT * total[2 * t + 1 : 2 * t + 2] / zc_ref[t : t + 1]
        )
    for make, k, table, i in sends:
        @pl.when(exists(table[i]))
        def _():
            make(k, i).wait_send()
    for copy in gy_copies + gx_copies:
        copy.wait_send()


def local(
    cotangent, section_states, inverse_area, edge_length, roughness, soil_conductance, zone_friction,
    zone_conductivity, wet_mask, element_zone, send_face, send_count, face_partner, volume_matrix, flux_in, flux_out,
):
    vmem = pl.BlockSpec(memory_space=pltpu.VMEM)
    arrays = (
        cotangent.reshape(42, 8, 128),
        section_states.reshape(3, 42, 1024),
        inverse_area.reshape(8, 128),
        edge_length.reshape(3, 8, 128),
        roughness.reshape(8, 128),
        soil_conductance.reshape(8, 128),
        zone_friction.reshape(4, 128),
        zone_conductivity.reshape(4, 128),
        wet_mask.reshape(8, 128),
        element_zone.reshape(8, 128),
        send_face.reshape(8, 256),
        face_partner.reshape(3, 8, 128),
        volume_matrix,
        flux_in,
        flux_out,
    )
    adjoint, grads = pl.pallas_call(
        kernel,
        out_shape=(
            jax.ShapeDtypeStruct((42, 8, 128), F32),
            jax.ShapeDtypeStruct((2, ZONES), F32),
        ),
        in_specs=[pl.BlockSpec(memory_space=pl.ANY)] * 15,
        out_specs=(vmem, vmem),
        scratch_shapes=[
            pltpu.VMEM((42, 8, 128), F32),
            pltpu.VMEM((3, 42, 1024), jnp.bfloat16),
            pltpu.VMEM((8, 128), F32),
            pltpu.VMEM((3, 8, 128), F32),
            pltpu.VMEM((8, 128), F32),
            pltpu.VMEM((8, 128), F32),
            pltpu.VMEM((4, 128), F32),
            pltpu.VMEM((4, 128), F32),
            pltpu.VMEM((8, 128), jnp.int32),
            pltpu.VMEM((8, 128), jnp.int32),
            pltpu.VMEM((8, 256), jnp.int32),
            pltpu.VMEM((3, 8, 128), jnp.int32),
            pltpu.VMEM((12, 12), F32),
            pltpu.VMEM((8, 8), F32),
            pltpu.VMEM((8, 8), F32),
            pltpu.VMEM((144, 8, 128), F32),
            pltpu.VMEM((64, 8, 128), F32),
            pltpu.VMEM((64, 8, 128), F32),
            pltpu.VMEM((48, 8, 128), F32),
            pltpu.VMEM((24, 8, 128), F32),
            pltpu.VMEM((3, 42, 8, 128), F32),
            pltpu.VMEM((3, 30, 8, 128), F32),
            pltpu.VMEM((3, 20, 8, 128), F32),
            pltpu.VMEM((42, 8, 128), F32),
            pltpu.VMEM((2, 42, 8, 128), F32),
            pltpu.VMEM((9, 8, 128), F32),
            pltpu.VMEM((4, 4, 30, 2, 128), F32),
            pltpu.VMEM((4, 4, 30, 2, 128), F32),
            pltpu.VMEM((4, 8, 128), F32),
            pltpu.VMEM((4, 4, 8, 128), F32),
            pltpu.VMEM((4, 2, 16, 128), F32),
            pltpu.VMEM((GY, 8, 128), F32),
            pltpu.VMEM((GX, 8, 128), F32),
            pltpu.SemaphoreType.DMA((15,)),
            pltpu.SemaphoreType.DMA((4, 12)),
            pltpu.SemaphoreType.DMA((4, 12)),
            pltpu.SemaphoreType.DMA((GY,)),
            pltpu.SemaphoreType.DMA((GY,)),
            pltpu.SemaphoreType.DMA((GX,)),
            pltpu.SemaphoreType.DMA((GX,)),
        ],
        compiler_params=pltpu.CompilerParams(
            collective_id=0, has_side_effects=True, vmem_limit_bytes=32 << 20
        ),
        name="sections",
    )(*[pltpu.with_memory_space_constraint(array, pltpu.MemorySpace.HBM) for array in arrays])
    return adjoint.reshape(1, 1, 42, 1024), grads


def solution(mesh):
    placed = (
        P("gx", "gy", None, None),
        P(None, "gx", "gy", None, None),
        P("gx", "gy", None),
        P("gx", "gy", None, None),
        P("gx", "gy", None),
        P("gx", "gy", None),
        P(),
        P(),
        P("gx", "gy", None),
        P("gx", "gy", None),
        P("gx", "gy", None, None),
        P("gx", "gy", None),
        P("gx", "gy", None, None),
        P(),
        P(),
        P(),
    )
    return jax.shard_map(
        local,
        mesh=mesh,
        in_specs=placed,
        out_specs=(P("gx", "gy", None, None), P()),
        check_vma=False,
    )
```

```python
import jax
import jax.numpy as jnp
from jax import lax
from jax.experimental import pallas as pl
from jax.experimental.pallas import tpu as pltpu
from jax.sharding import PartitionSpec as P

GX, GY = 16, 8
COMPS = 14
QCOMP, ZCOMP = 14, 15
ZONES = 512
DT = 0.2
GRAD_WEIGHT = 1.0 / 64.0
SPLIT = 7
FIRST = 2 + 2 * SPLIT
FACE_NODES = ((1, 2), (2, 0), (0, 1))
MAIN = (1, 3, 4, 6)
DIAG = (0, 2, 5, 7)
STEPS = ((-1, -1), (-1, 0), (-1, 1), (0, -1), (0, 1), (1, -1), (1, 0), (1, 1))
WINDOW, BEHIND = 88, 40
MESH = pl.DeviceIdType.MESH
TILE = (8, 128)
F32 = jnp.float32


LOOKUP = lax.GatherDimensionNumbers(
    offset_dims=(), collapsed_slice_dims=(1,), start_index_map=(1,), operand_batching_dims=(0,),
    start_indices_batching_dims=(0,),
)


def lanes_of(idx):
    return idx.reshape(8, 128, 1)


def take(x, idx):
    return lax.gather(
        x, idx, LOOKUP, slice_sizes=(1, 1), mode=lax.GatherScatterMode.PROMISE_IN_BOUNDS
    )


def row(ref, *at):
    return jnp.broadcast_to(ref[at], TILE)


def pick(code, values, like):
    out = jnp.full(TILE, values[-1], like.dtype)
    for i in range(len(values) - 2, -1, -1):
        out = jnp.where(code == i, values[i], out)
    return out


def ends(nodes, is0, is1):
    a, b, c = nodes
    first = lax.select(is0, b, lax.select(is1, c, a))
    second = lax.select(is0, c, lax.select(is1, a, b))
    return first, second


def kernel(
    cot_hbm, states_hbm, area_hbm, edge_hbm, rough_hbm, soil_hbm, zf_hbm, zc_hbm, wet_hbm, zone_hbm, send_hbm,
    partner_hbm, vol_hbm, fin_hbm, fout_hbm,
    out, grads,
    cot, states, area_ref, edge_ref, rough_ref, soil_ref, zf_ref, zc_ref, wet_ref, zone_ref, send_ref, partner_ref,
    vol_ref, fin_ref, fout_ref, vol, fin, fout,
    tab, aux, xs, local, fwd, pre, lam, kept, sbuf, rbuf, sdiag, rdiag, cdiag, gyb, gxb,
    in_sem, send_sem, recv_sem, gy_send, gy_recv, gx_send, gx_recv,
):
    ix, iy = lax.axis_index("gx"), lax.axis_index("gy")

    def at(dx, dy):
        return (lax.rem(ix + dx + GX, GX), lax.rem(iy + dy + GY, GY))

    side_x = {-1: (ix + GX - 1) // GX, 0: 1, 1: (2 * GX - 2 - ix) // GX}
    side_y = {-1: (iy + GY - 1) // GY, 0: 1, 1: (2 * GY - 2 - iy) // GY}

    def exists(n):
        dx, dy = STEPS[n]
        return side_x[dx] * side_y[dy] == 1

    barrier = pltpu.get_barrier_semaphore()
    peers = [at(k, 0) for k in (1, 15)] + [at(0, k) for k in (1, 7)]
    peers += [at(k, 0) for k in (8, 7, 9, 6, 10, 5, 11, 4, 12, 3, 13, 2, 14)]
    peers += [at(0, k) for k in (4, 3, 5, 2, 6)]
    for n in DIAG:
        @pl.when(exists(n))
        def _():
            pl.semaphore_signal(barrier, inc=1, device_id=at(*STEPS[n]), device_id_type=MESH)
    for peer in peers:
        pl.semaphore_signal(barrier, inc=1, device_id=peer, device_id_type=MESH)
    greeters = len(peers) + (side_x[-1] + side_x[1]) * (side_y[-1] + side_y[1])

    inputs = (
        (cot_hbm, cot), (states_hbm, states), (area_hbm, area_ref), (edge_hbm, edge_ref), (rough_hbm, rough_ref),
        (soil_hbm, soil_ref), (zf_hbm, zf_ref), (zc_hbm, zc_ref), (wet_hbm, wet_ref), (zone_hbm, zone_ref),
        (send_hbm, send_ref), (partner_hbm, partner_ref), (vol_hbm, vol_ref), (fin_hbm, fin_ref), (fout_hbm, fout_ref),
    )
    reads = [pltpu.make_async_copy(src, dst, in_sem.at[i]) for i, (src, dst) in enumerate(inputs)]
    for read in reads:
        read.start()
    for read in reads:
        read.wait()

    sub = lax.broadcasted_iota(jnp.int32, TILE, 0)
    lane = lax.broadcasted_iota(jnp.int32, TILE, 1)

    lane16 = [(lane >> 4) == g for g in range(4)]
    lane4 = [((lane >> 2) & 3) == d for d in range(4)]
    area = area_ref[...]
    rough = rough_ref[...]
    wet = wet_ref[...].astype(F32)
    zone = zone_ref[...]
    edge = [edge_ref[f] for f in range(3)]
    kappa = jnp.zeros(TILE, F32)
    zfric = jnp.zeros(TILE, F32)
    zlane, zhi = lanes_of(zone & 127), zone >> 7
    for t in range(4):
        kappa = jnp.where(zhi == t, take(row(zc_ref, pl.ds(t, 1)), zlane), kappa)
        zfric = jnp.where(zhi == t, take(row(zf_ref, pl.ds(t, 1)), zlane), zfric)
    kappa = kappa * soil_ref[...]
    half_kappa = 0.5 * kappa
    rough_zone = zfric * rough

    slots = jnp.concatenate(
        [send_ref[n : n + 1, h * 128 : (h + 1) * 128] for n in MAIN for h in range(2)], axis=0
    )
    m_lo, m_f = lanes_of(slots & 127), slots >> 10
    m_hi = [((slots >> 7) & 7) == t for t in range(8)]
    m_is0, m_is1 = m_f == 0, m_f == 1
    dslots = jnp.zeros(TILE, jnp.int32)
    for i, n in enumerate(DIAG):
        first = jnp.broadcast_to(send_ref[n : n + 1, 0:128], TILE)
        d = 3 - i
        moved = pltpu.roll(first, 4 * d, axis=1) if d else first
        dslots = jnp.where((lane >> 2) == d, moved, dslots)
    d_lo, d_f = lanes_of(dslots & 127), dslots >> 10
    d_hi = [((dslots >> 7) & 7) == t for t in range(8)]
    d_is0, d_is1 = d_f == 0, d_f == 1

    p_lo, p_loc, p_rem, p_is0, p_is1 = [], [], [], [], []
    for f in range(3):
        p = partner_ref[f]
        there = p - 3072
        n = there >> 8
        slot_row = pick(n, (8, 0, 8, 2, 4, 8, 6, 8), p) + ((there >> 7) & 1)
        is_diag = (n == 0) | (n == 2) | (n == 5) | (n == 7)
        far = p >= 3072
        d_lane = pick(n, (0, 0, 4, 0, 0, 8, 0, 12), p) + (p & 3)
        p_lo.append(lanes_of(jnp.where(far & is_diag, d_lane, p & 127)))
        chunk = jnp.where(far, -1, (p >> 7) & 7)
        p_loc.append([chunk == t for t in range(8)])
        chunk = jnp.where(far, jnp.where(is_diag, 8, slot_row), -1)
        p_rem.append([chunk == t for t in range(9)])
        p_is0.append((p >> 10) == 0)
        p_is1.append((p >> 10) == 1)

    def from_slots(ref, c):
        nodes = []
        for n in range(3):
            acc = jnp.zeros(TILE, F32)
            for s in range(8):
                acc = lax.select(m_hi[s], take(row(ref, c * 3 + n, pl.ds(s, 1)), m_lo), acc)
            nodes.append(acc)
        return ends(nodes, m_is0, m_is1)

    def from_partner(ref, c, f):
        nodes = []
        for n in range(3):
            acc = jnp.zeros(TILE, F32)
            for s in range(8):
                acc = lax.select(p_loc[f][s], take(row(ref, c * 3 + n, pl.ds(s, 1)), p_lo[f]), acc)
            nodes.append(acc)
        return ends(nodes, p_is0[f], p_is1[f])

    def from_diag(ref, first, count):
        rows = ref.shape[0]
        flat = ref.reshape(rows * 8, 128)
        parts = []
        for h in range(count):
            nodes = []
            for n in range(3):
                acc = jnp.zeros(TILE, F32)
                for s in range(8):
                    got = flat[pl.ds(((first + h * 8) * 3 + n) * 8 + s, 8, stride=24), :]
                    acc = lax.select(d_hi[s], take(got, d_lo), acc)
                nodes.append(acc)
            parts.append(ends(nodes, d_is0, d_is1))
        return parts

    for f in range(3):
        aux[FACE_NODES[f][0]] = edge[f]
        aux[3 + f] = half_kappa
    for r in range(6, 24):
        aux[r] = jnp.zeros(TILE, F32)
    for r in range(45, 48):
        tab[r] = zone.astype(F32)
    slot_edge = from_slots(aux, 0)[0]
    slot_kedge = from_slots(aux, 1)[0] * slot_edge
    d_aux = from_diag(aux, 0, 1)[0][0]
    d_edge = jnp.broadcast_to(d_aux[0:1], TILE)
    d_kedge = jnp.broadcast_to(d_aux[1:2], TILE) * d_edge
    d_scale = [jnp.where(sub < 4, d_edge, d_kedge), jnp.where(sub < 6, d_kedge, 1.0)]
    kedge = [half_kappa * edge[f] for f in range(3)]

    sends = []

    def remote(src, dst, ssem, rsem, n):
        return pltpu.make_async_remote_copy(
            src_ref=src, dst_ref=dst, send_sem=ssem, recv_sem=rsem, device_id=at(*STEPS[n]), device_id_type=MESH
        )

    def part_copy(k, i, rows, a):
        return remote(
            sbuf.at[k, i, rows], rbuf.at[k, 3 - i, rows], send_sem.at[k, a + i], recv_sem.at[k, a + 3 - i], MAIN[i]
        )

    def first_copy(k, i):
        return part_copy(k, i, pl.ds(0, FIRST), 0)

    def second_copy(k, i):
        return part_copy(k, i, pl.ds(FIRST, 30 - FIRST), 8)

    def forward_copy(k, i):
        return part_copy(k, i, pl.ds(0, 20), 0)

    def diag_copy(k, i):
        return remote(
            sdiag.at[k], rdiag.at[k, 3 - i], send_sem.at[k, 4 + i], recv_sem.at[k, 7 - i], DIAG[i]
        )

    def send(make, k, table, order):
        for i in order:
            @pl.when(exists(table[i]))
            def _():
                make(k, i).start()
            sends.append((make, k, table, i))

    def arrive(make, k, table, which):
        for i in which:
            @pl.when(exists(table[i]))
            def _():
                make(k, 3 - i).wait_recv()

    def fill_slots(k, ref, comps, first_channel, scales):
        for c in comps:
            pair = from_slots(ref, c)
            for j in range(2 if c < COMPS else 1):
                value = pair[j] * scales(c) if c < COMPS and scales else pair[j]
                ch = c * 2 + j + first_channel if c < COMPS else c - COMPS
                for d in range(4):
                    sbuf[k, d, ch] = value[2 * d : 2 * d + 2]

    def unpack_state(m):
        flat = xs.at[m].reshape(42 * 8, 128)
        for s in range(8):
            flat[pl.ds(s, 42, stride=8), :] = states[m, :, s * 128 : (s + 1) * 128].astype(F32)

    def pack_diag(k, halves, scales):
        packed = jnp.zeros(TILE, F32)
        for j in range(2):
            for h in range(2):
                g = 2 * j + h
                value = halves[h][j] * scales[h] if scales else halves[h][j]
                packed = lax.select(lane16[g], pltpu.roll(value, 16 * g, axis=1) if g else value, packed)
        sdiag[k] = packed
        send(diag_copy, k, DIAG, (0, 1, 2, 3))

    def merge_diag(k):
        acc = rdiag[k, 0]
        for d in range(1, 4):
            acc = lax.select(lane4[d], rdiag[k, d], acc)
        for j in range(2):
            for h in range(2):
                g = 2 * j + h
                cdiag[k, j, h * 8 : h * 8 + 8] = pltpu.roll(acc, 128 - 16 * g, axis=1) if g else acc

    def receive(k, ref, channels, rows):
        for f in range(3):
            for ch in channels:
                acc = ref[f, ch]
                for s in rows:
                    acc = lax.select(
                        p_rem[f][s], take(row(rbuf, k, s // 2, ch, pl.ds(s % 2, 1)), p_lo[f]), acc
                    )
                ref[f, ch] = acc

    def receive_diag(k, ref, f, ch, c, j):
        return lax.select(p_rem[f][8], take(row(cdiag, k, j, pl.ds(c, 1)), p_lo[f]), ref[f, ch])

    base = 4 * (ix * GY + iy)

    def relative(ids):
        return (ids - base + (BEHIND + ZONES)) & (ZONES - 1)

    tf = jnp.zeros(TILE, F32)
    tc = jnp.zeros(TILE, F32)
    far_terms = [jnp.zeros(TILE, F32)] * 3
    weights = {2: 2.0 / 3.0, 1: 0.25, 0: 1.0}
    FWD = 3

    def own_terms(k, v, x, weight, tf, tc):
        moment = jnp.sqrt(1.0 + (1.0 / 6.0) * sum(x[r] * x[r] for r in range(3, 9)))
        acc = jnp.zeros(TILE, F32)
        for r in range(3, 9):
            acc = acc + v[r] * x[r]
        tf = tf - weight * (wet * rough * moment) * acc
        flows = jnp.zeros(TILE, F32)
        faces = jnp.zeros(TILE, F32)
        for n in range(3):
            above = v[12 + n] - 0.5 * wet * v[9 + n]
            flows = flows + above * (x[9 + n] - x[12 + n])
            acc = tab[12 + n] * x[12 + n]
            for l in range(10):
                r = 12 + l * 3 + n
                if l:
                    acc = acc + tab[r] * x[r]
                if l < 9:
                    flows = flows + (v[r + 3] - v[r]) * (x[r] - x[r + 3])
            faces = faces + sum(kedge[f] for f in range(3) if n in FACE_NODES[f]) * acc
        tc = tc + weight * (kappa * flows - faces)
        return tf, tc, wet * rough_zone * moment

    def zone_bins(tf, tc):
        bins_f = jnp.zeros(TILE, F32)
        bins_c = [jnp.zeros(TILE, F32) for _ in range(WINDOW // 8)]
        none = jnp.zeros(TILE, F32)
        own_rel = relative(zone)
        far_rel = [relative(kept[6 + f].astype(jnp.int32)) for f in range(3)]
        for s in range(8):
            rel = jnp.broadcast_to(own_rel[s : s + 1], TILE) - sub
            tf_row = jnp.broadcast_to(tf[s : s + 1], TILE)
            tc_row = jnp.broadcast_to(tc[s : s + 1], TILE)
            hit = rel == BEHIND
            bins_f = bins_f + lax.select(hit, tf_row, none)
            bins_c[BEHIND // 8] = bins_c[BEHIND // 8] + lax.select(hit, tc_row, none)
            for f in range(3):
                rel = jnp.broadcast_to(far_rel[f][s : s + 1], TILE) - sub
                term = jnp.broadcast_to(far_terms[f][s : s + 1], TILE)
                for z in (0, 1, 2, 4, 5, 6, 8, 9, 10):
                    bins_c[z] = bins_c[z] + lax.select(rel == 8 * z, term, none)
        rows = jnp.concatenate(bins_c + [bins_f] + [none] * (15 - WINDOW // 8), axis=0)
        sums = lax.dot_general(
            jnp.ones(TILE, F32), rows, (((1,), (1,)), ((), ())),
            precision=lax.Precision.HIGHEST, preferred_element_type=F32,
        )
        rel = relative((sub >> 1) * 128 + lane)
        is_friction = (sub & 1) == 0
        own_zone = (rel >= BEHIND) & (rel < BEHIND + 8)
        found = take(sums, lanes_of(jnp.where(is_friction, rel + (WINDOW - BEHIND), rel) & 127))
        return jnp.where(is_friction, jnp.where(own_zone, found, 0.0), jnp.where(rel < WINDOW, found, 0.0))

    gy_copies = [
        pltpu.make_async_remote_copy(
            src_ref=gyb.at[iy], dst_ref=gyb.at[iy], send_sem=gy_send.at[d], recv_sem=gy_recv.at[d],
            device_id=at(0, d), device_id_type=MESH,
        )
        for d in (4, 3, 5, 2, 6, 1, 7)
    ]
    gx_copies = [
        pltpu.make_async_remote_copy(
            src_ref=gxb.at[ix], dst_ref=gxb.at[ix], send_sem=gx_send.at[d], recv_sem=gx_recv.at[d],
            device_id=at(d, 0), device_id_type=MESH,
        )
        for d in (8, 6, 10, 7, 9, 5, 11, 4, 12, 3, 13, 2, 14, 1, 15)
    ]

    for k in (2, 1, 0):
        v = cot if k == 2 else lam.at[k]
        weight = weights[k] * DT
        x = xs.at[k]
        if k == 2:
            unpack_state(2)
        squares = []
        for n in range(3):
            squares.append(sum(x[c * 3 + n] * x[c * 3 + n] for c in range(4)))
        q = [squares[a] + squares[b] for a, b in FACE_NODES]
        for f in range(3):
            tab[42 + FACE_NODES[f][0]] = q[f]
        wet_area = wet * area
        for r in range(12):
            tab[r] = wet_area * v[r]
        for r in range(12, 42):
            tab[r] = area * v[r]

        if k == 0:
            tf, tc, wet_friction = own_terms(k, v, x, weight, tf, tc)
            for f in range(3):
                term = jnp.zeros(TILE, F32)
                for ch in range(8, 28):
                    r = 12 + ((ch - 8) // 2) * 3 + FACE_NODES[f][ch % 2]
                    term = term + fwd[f, ch - 8] * tab[r]
                tc = tc + weight * kedge[f] * term
            gyb[iy] = zone_bins(tf, tc)
            for copy in gy_copies:
                copy.start()

        last = ZCOMP if k == 2 else QCOMP
        if k < 2:
            pack_diag(k, from_diag(tab, 0, 2), d_scale)
        slot_scale = lambda c: slot_edge if c < 4 else slot_kedge
        fill_slots(k, tab, list(range(COMPS, last + 1)) + list(range(SPLIT)), 2, slot_scale)
        if k == 2:
            halves = from_diag(tab, 0, 2)
            pl.semaphore_wait(barrier, greeters)
            pack_diag(k, halves, d_scale)
        send(first_copy, k, MAIN, (0, 3, 1, 2))
        fill_slots(k, tab, range(SPLIT, COMPS), 2, slot_scale)
        send(second_copy, k, MAIN, (0, 3, 1, 2))

        if k == 2:
            for m in (0, 1):
                unpack_state(m)
            for small, wide, size in ((vol_ref, vol, 12), (fin_ref, fin, 8), (fout_ref, fout, 8)):
                for b in range(size):
                    for a in range(size):
                        wide[b * size + a] = jnp.broadcast_to(small[b : b + 1, a : a + 1], TILE)

        if k == 2:
            for f in range(3):
                outer_edge = from_partner(aux, 0, f)[0]
                kept[f] = outer_edge
                kept[3 + f] = from_partner(aux, 1, f)[0] * outer_edge
        for f in range(3):
            for c in range(last + 1):
                pair = from_partner(tab, c, f)
                if c < COMPS:
                    scale = kept[f] if c < 4 else kept[3 + f]
                    local[f, c * 2 + 2] = pair[0] * scale
                    local[f, c * 2 + 3] = pair[1] * scale
                else:
                    local[f, c - COMPS] = pair[0]

        if k > 0:
            tf, tc, wet_friction = own_terms(k, v, x, weight, tf, tc)
        bars = [None] * 12
        for r in range(12):
            bars[r] = sum(vol[b * 12 + r] * tab[b] for b in range(12))
            if 3 <= r < 9:
                bars[r] = bars[r] - wet_friction * v[r]
        for f in range(3):
            for a in range(8):
                total = sum(
                    fin[b * 8 + a] * tab[(b // 2) * 3 + FACE_NODES[f][b % 2]] for b in range(8)
                )
                r = (a // 2) * 3 + FACE_NODES[f][a % 2]
                bars[r] = bars[r] + edge[f] * total
        for n in range(3):
            node_edge = sum(kedge[f] for f in range(3) if n in FACE_NODES[f])
            above = v[12 + n] - 0.5 * wet * v[9 + n]
            bars[9 + n] = bars[9 + n] + kappa * above
            for l in range(10):
                r = 12 + l * 3 + n
                below = v[r + 3] - v[r] if l < 9 else 0.0
                pre[r] = kappa * (below - above) - node_edge * tab[r]
                above = below
        for r in range(12):
            pre[r] = bars[r]

        if k == 2:
            halves = from_diag(xs.at[0], 4, 1) + from_diag(xs.at[0], 6, 1)
            pack_diag(FWD, halves, None)
            fill_slots(FWD, xs.at[0], range(4, COMPS), -8, None)
            send(forward_copy, FWD, MAIN, (0, 3, 1, 2))
            for f in range(3):
                for c in range(4, COMPS):
                    pair = from_partner(xs.at[0], c, f)
                    fwd[f, c * 2 - 8] = pair[0]
                    fwd[f, c * 2 - 7] = pair[1]
        if k == 1:
            arrive(forward_copy, FWD, MAIN, range(4))
            arrive(diag_copy, FWD, DIAG, range(4))
            merge_diag(FWD)
            receive(FWD, fwd, range(20), range(8))
            for f in range(3):
                for ch in range(20):
                    c = ch // 2 if ch < 4 else ch // 2 + 6
                    fwd[f, ch] = receive_diag(FWD, fwd, f, ch, c, ch % 2)
        if k == 0:
            for copy in gy_copies:
                copy.wait_recv()
            total = gyb[0]
            for i in range(1, GY):
                total = total + gyb[i]
            gxb[ix] = total
            for copy in gx_copies:
                copy.start()

        early = [ch for ch in range(FIRST) if ch != 1 or k == 2]
        late = range(FIRST, 30)
        terms = [jnp.zeros(TILE, F32)] * 3

        def porewater(f, channels):
            for ch in channels:
                r = 12 + ((ch - 10) // 2) * 3 + FACE_NODES[f][ch % 2]
                value = receive_diag(k, local, f, ch, ch // 2 - 1, ch % 2)
                if k > 0:
                    terms[f] = terms[f] + value * x[r]
                pre[r] = pre[r] + value

        arrive(first_copy, k, MAIN, (1, 2))
        receive(k, local, early, range(2, 6))
        arrive(second_copy, k, MAIN, (1, 2))
        receive(k, local, late, range(2, 6))
        arrive(first_copy, k, MAIN, (0, 3))
        receive(k, local, early, (0, 1, 6, 7))
        arrive(diag_copy, k, DIAG, range(4))
        merge_diag(k)
        for f in range(3):
            if k == 2:
                kept[6 + f] = receive_diag(k, local, f, 1, ZCOMP, 0)
            outer_q = receive_diag(k, local, f, 0, QCOMP, 0)
            half_speed = 0.5 * jnp.sqrt(1.0 + 0.03125 * (q[f] + outer_q))
            outer = [receive_diag(k, local, f, a + 2, a // 2, a % 2) for a in range(8)]
            for a in range(8):
                r = (a // 2) * 3 + FACE_NODES[f][a % 2]
                total = half_speed * (edge[f] * tab[r] - outer[a])
                for b in range(8):
                    total = total - fout[b * 8 + a] * outer[b]
                pre[r] = pre[r] + total
            porewater(f, range(10, FIRST))
        arrive(second_copy, k, MAIN, (0, 3))
        receive(k, local, late, (0, 1, 6, 7))
        for f in range(3):
            porewater(f, late)
            far_terms[f] = far_terms[f] + weight * terms[f]

        for r in range(42):
            if k == 2:
                lam[1, r] = (2.0 / 3.0) * (cot[r] + DT * pre[r])
            elif k == 1:
                lam[0, r] = 0.25 * (lam[1, r] + DT * pre[r])
            else:
                out[r] = cot[r] * (1.0 / 3.0) + 0.75 * lam[1, r] + lam[0, r] + DT * pre[r]

    for copy in gx_copies:
        copy.wait_recv()
    total = gxb[0]
    for i in range(1, GX):
        total = total + gxb[i]
    for t in range(4):
        grads[0:1, t * 128 : (t + 1) * 128] = GRAD_WEIGHT * total[2 * t : 2 * t + 1]
        grads[1:2, t * 128 : (t + 1) * 128] = (
            GRAD_WEIGHT * total[2 * t + 1 : 2 * t + 2] / zc_ref[t : t + 1]
        )
    for make, k, table, i in sends:
        @pl.when(exists(table[i]))
        def _():
            make(k, i).wait_send()
    for copy in gy_copies + gx_copies:
        copy.wait_send()


def deliver(adjoint, grads, adjoint_out, grads_out, sem):
    first = pltpu.make_async_copy(adjoint, adjoint_out, sem.at[0])
    second = pltpu.make_async_copy(grads, grads_out, sem.at[1])
    first.start()
    second.start()
    first.wait()
    second.wait()


def local(
    cotangent, section_states, inverse_area, edge_length, roughness, soil_conductance, zone_friction,
    zone_conductivity, wet_mask, element_zone, send_face, send_count, face_partner, volume_matrix, flux_in, flux_out,
):
    vmem = pl.BlockSpec(memory_space=pltpu.VMEM)
    arrays = (
        cotangent.reshape(42, 8, 128),
        section_states.reshape(3, 42, 1024),
        inverse_area.reshape(8, 128),
        edge_length.reshape(3, 8, 128),
        roughness.reshape(8, 128),
        soil_conductance.reshape(8, 128),
        zone_friction.reshape(4, 128),
        zone_conductivity.reshape(4, 128),
        wet_mask.reshape(8, 128),
        element_zone.reshape(8, 128),
        send_face.reshape(8, 256),
        face_partner.reshape(3, 8, 128),
        volume_matrix,
        flux_in,
        flux_out,
    )
    adjoint, grads = pl.pallas_call(
        kernel,
        out_shape=(
            jax.ShapeDtypeStruct((42, 8, 128), F32),
            jax.ShapeDtypeStruct((2, ZONES), F32),
        ),
        in_specs=[pl.BlockSpec(memory_space=pl.ANY)] * 15,
        out_specs=(vmem, vmem),
        scratch_shapes=[
            pltpu.VMEM((42, 8, 128), F32),
            pltpu.VMEM((3, 42, 1024), jnp.bfloat16),
            pltpu.VMEM((8, 128), F32),
            pltpu.VMEM((3, 8, 128), F32),
            pltpu.VMEM((8, 128), F32),
            pltpu.VMEM((8, 128), F32),
            pltpu.VMEM((4, 128), F32),
            pltpu.VMEM((4, 128), F32),
            pltpu.VMEM((8, 128), jnp.int32),
            pltpu.VMEM((8, 128), jnp.int32),
            pltpu.VMEM((8, 256), jnp.int32),
            pltpu.VMEM((3, 8, 128), jnp.int32),
            pltpu.VMEM((12, 12), F32),
            pltpu.VMEM((8, 8), F32),
            pltpu.VMEM((8, 8), F32),
            pltpu.VMEM((144, 8, 128), F32),
            pltpu.VMEM((64, 8, 128), F32),
            pltpu.VMEM((64, 8, 128), F32),
            pltpu.VMEM((48, 8, 128), F32),
            pltpu.VMEM((24, 8, 128), F32),
            pltpu.VMEM((3, 42, 8, 128), F32),
            pltpu.VMEM((3, 30, 8, 128), F32),
            pltpu.VMEM((3, 20, 8, 128), F32),
            pltpu.VMEM((42, 8, 128), F32),
            pltpu.VMEM((2, 42, 8, 128), F32),
            pltpu.VMEM((9, 8, 128), F32),
            pltpu.VMEM((4, 4, 30, 2, 128), F32),
            pltpu.VMEM((4, 4, 30, 2, 128), F32),
            pltpu.VMEM((4, 8, 128), F32),
            pltpu.VMEM((4, 4, 8, 128), F32),
            pltpu.VMEM((4, 2, 16, 128), F32),
            pltpu.VMEM((GY, 8, 128), F32),
            pltpu.VMEM((GX, 8, 128), F32),
            pltpu.SemaphoreType.DMA((15,)),
            pltpu.SemaphoreType.DMA((4, 12)),
            pltpu.SemaphoreType.DMA((4, 12)),
            pltpu.SemaphoreType.DMA((GY,)),
            pltpu.SemaphoreType.DMA((GY,)),
            pltpu.SemaphoreType.DMA((GX,)),
            pltpu.SemaphoreType.DMA((GX,)),
        ],
        compiler_params=pltpu.CompilerParams(
            collective_id=0, has_side_effects=True, vmem_limit_bytes=32 << 20
        ),
        name="sections",
    )(*[pltpu.with_memory_space_constraint(array, pltpu.MemorySpace.HBM) for array in arrays])
    adjoint, grads = pl.pallas_call(
        deliver,
        out_shape=(
            jax.ShapeDtypeStruct((42, 8, 128), F32),
            jax.ShapeDtypeStruct((2, ZONES), F32),
        ),
        in_specs=[vmem, vmem],
        out_specs=(pl.BlockSpec(memory_space=pltpu.MemorySpace.HBM),) * 2,
        scratch_shapes=[pltpu.SemaphoreType.DMA((2,))],
        name="deliver",
    )(*[pltpu.with_memory_space_constraint(array, pltpu.MemorySpace.VMEM) for array in (adjoint, grads)])
    return adjoint.reshape(1, 1, 42, 1024), grads


def solution(mesh):
    placed = (
        P("gx", "gy", None, None),
        P(None, "gx", "gy", None, None),
        P("gx", "gy", None),
        P("gx", "gy", None, None),
        P("gx", "gy", None),
        P("gx", "gy", None),
        P(),
        P(),
        P("gx", "gy", None),
        P("gx", "gy", None),
        P("gx", "gy", None, None),
        P("gx", "gy", None),
        P("gx", "gy", None, None),
        P(),
        P(),
        P(),
    )
    return jax.shard_map(
        local,
        mesh=mesh,
        in_specs=placed,
        out_specs=(P("gx", "gy", None, None), P()),
        check_vma=False,
    )
```

```python
import jax
import jax.numpy as jnp
from jax import lax
from jax.experimental import pallas as pl
from jax.experimental.pallas import tpu as pltpu
from jax.sharding import PartitionSpec as P

GX, GY = 16, 8
COMPS = 14
QCOMP, ZCOMP = 14, 15
ZONES = 512
DT = 0.2
GRAD_WEIGHT = 1.0 / 64.0
SPLIT = 7
FIRST = 2 + 2 * SPLIT
FACE_NODES = ((1, 2), (2, 0), (0, 1))
MAIN = (1, 3, 4, 6)
DIAG = (0, 2, 5, 7)
STEPS = ((-1, -1), (-1, 0), (-1, 1), (0, -1), (0, 1), (1, -1), (1, 0), (1, 1))
WINDOW, BEHIND = 88, 40
MESH = pl.DeviceIdType.MESH
TILE = (8, 128)
F32 = jnp.float32


LOOKUP = lax.GatherDimensionNumbers(
    offset_dims=(), collapsed_slice_dims=(1,), start_index_map=(1,), operand_batching_dims=(0,),
    start_indices_batching_dims=(0,),
)


def lanes_of(idx):
    return idx.reshape(8, 128, 1)


def take(x, idx):
    return lax.gather(
        x, idx, LOOKUP, slice_sizes=(1, 1), mode=lax.GatherScatterMode.PROMISE_IN_BOUNDS
    )


def row(ref, *at):
    return jnp.broadcast_to(ref[at], TILE)


def pick(code, values, like):
    out = jnp.full(TILE, values[-1], like.dtype)
    for i in range(len(values) - 2, -1, -1):
        out = jnp.where(code == i, values[i], out)
    return out


def ends(nodes, is0, is1):
    a, b, c = nodes
    first = lax.select(is0, b, lax.select(is1, c, a))
    second = lax.select(is0, c, lax.select(is1, a, b))
    return first, second


def kernel(
    cot_hbm, states_hbm, area_hbm, edge_hbm, rough_hbm, soil_hbm, zf_hbm, zc_hbm, wet_hbm, zone_hbm, send_hbm,
    partner_hbm, vol_hbm, fin_hbm, fout_hbm,
    out, grads,
    cot, states, area_ref, edge_ref, rough_ref, soil_ref, zf_ref, zc_ref, wet_ref, zone_ref, send_ref, partner_ref,
    vol_ref, fin_ref, fout_ref, vol, fin, fout,
    tab, aux, xs, local, fwd, pre, lam, kept, sbuf, rbuf, sdiag, rdiag, cdiag, gyb, gxb,
    in_sem, send_sem, recv_sem, gy_send, gy_recv, gx_send, gx_recv,
):
    ix, iy = lax.axis_index("gx"), lax.axis_index("gy")

    def at(dx, dy):
        return (lax.rem(ix + dx + GX, GX), lax.rem(iy + dy + GY, GY))

    side_x = {-1: (ix + GX - 1) // GX, 0: 1, 1: (2 * GX - 2 - ix) // GX}
    side_y = {-1: (iy + GY - 1) // GY, 0: 1, 1: (2 * GY - 2 - iy) // GY}

    def exists(n):
        dx, dy = STEPS[n]
        return side_x[dx] * side_y[dy] == 1

    barrier = pltpu.get_barrier_semaphore()
    peers = [at(k, 0) for k in (1, 15)] + [at(0, k) for k in (1, 7)]
    peers += [at(k, 0) for k in (8, 7, 9, 6, 10, 5, 11, 4, 12, 3, 13, 2, 14)]
    peers += [at(0, k) for k in (4, 3, 5, 2, 6)]
    for n in DIAG:
        @pl.when(exists(n))
        def _():
            pl.semaphore_signal(barrier, inc=1, device_id=at(*STEPS[n]), device_id_type=MESH)
    for peer in peers:
        pl.semaphore_signal(barrier, inc=1, device_id=peer, device_id_type=MESH)
    greeters = len(peers) + (side_x[-1] + side_x[1]) * (side_y[-1] + side_y[1])

    inputs = (
        (cot_hbm, cot), (states_hbm, states), (area_hbm, area_ref), (edge_hbm, edge_ref), (rough_hbm, rough_ref),
        (soil_hbm, soil_ref), (zf_hbm, zf_ref), (zc_hbm, zc_ref), (wet_hbm, wet_ref), (zone_hbm, zone_ref),
        (send_hbm, send_ref), (partner_hbm, partner_ref), (vol_hbm, vol_ref), (fin_hbm, fin_ref), (fout_hbm, fout_ref),
    )
    reads = [pltpu.make_async_copy(src, dst, in_sem.at[i]) for i, (src, dst) in enumerate(inputs)]
    for read in reads:
        read.start()
    for read in reads:
        read.wait()

    sub = lax.broadcasted_iota(jnp.int32, TILE, 0)
    lane = lax.broadcasted_iota(jnp.int32, TILE, 1)

    lane16 = [(lane >> 4) == g for g in range(4)]
    lane4 = [((lane >> 2) & 3) == d for d in range(4)]
    area = area_ref[...]
    rough = rough_ref[...]
    wet = wet_ref[...].astype(F32)
    zone = zone_ref[...]
    edge = [edge_ref[f] for f in range(3)]
    kappa = jnp.zeros(TILE, F32)
    zfric = jnp.zeros(TILE, F32)
    zlane, zhi = lanes_of(zone & 127), zone >> 7
    for t in range(4):
        kappa = jnp.where(zhi == t, take(row(zc_ref, pl.ds(t, 1)), zlane), kappa)
        zfric = jnp.where(zhi == t, take(row(zf_ref, pl.ds(t, 1)), zlane), zfric)
    kappa = kappa * soil_ref[...]
    half_kappa = 0.5 * kappa
    rough_zone = zfric * rough

    slots = jnp.concatenate(
        [send_ref[n : n + 1, h * 128 : (h + 1) * 128] for n in MAIN for h in range(2)], axis=0
    )
    m_lo, m_f = lanes_of(slots & 127), slots >> 10
    m_hi = [((slots >> 7) & 7) == t for t in range(8)]
    m_is0, m_is1 = m_f == 0, m_f == 1
    dslots = jnp.zeros(TILE, jnp.int32)
    for i, n in enumerate(DIAG):
        first = jnp.broadcast_to(send_ref[n : n + 1, 0:128], TILE)
        d = 3 - i
        moved = pltpu.roll(first, 4 * d, axis=1) if d else first
        dslots = jnp.where((lane >> 2) == d, moved, dslots)
    d_lo, d_f = lanes_of(dslots & 127), dslots >> 10
    d_hi = [((dslots >> 7) & 7) == t for t in range(8)]
    d_is0, d_is1 = d_f == 0, d_f == 1

    p_lo, p_loc, p_rem, p_is0, p_is1 = [], [], [], [], []
    for f in range(3):
        p = partner_ref[f]
        there = p - 3072
        n = there >> 8
        slot_row = pick(n, (8, 0, 8, 2, 4, 8, 6, 8), p) + ((there >> 7) & 1)
        is_diag = (n == 0) | (n == 2) | (n == 5) | (n == 7)
        far = p >= 3072
        d_lane = pick(n, (0, 0, 4, 0, 0, 8, 0, 12), p) + (p & 3)
        p_lo.append(lanes_of(jnp.where(far & is_diag, d_lane, p & 127)))
        chunk = jnp.where(far, -1, (p >> 7) & 7)
        p_loc.append([chunk == t for t in range(8)])
        chunk = jnp.where(far, jnp.where(is_diag, 8, slot_row), -1)
        p_rem.append([chunk == t for t in range(9)])
        p_is0.append((p >> 10) == 0)
        p_is1.append((p >> 10) == 1)

    def from_slots(ref, c):
        nodes = []
        for n in range(3):
            acc = jnp.zeros(TILE, F32)
            for s in range(8):
                acc = lax.select(m_hi[s], take(row(ref, c * 3 + n, pl.ds(s, 1)), m_lo), acc)
            nodes.append(acc)
        return ends(nodes, m_is0, m_is1)

    def from_partner(ref, c, f):
        nodes = []
        for n in range(3):
            acc = jnp.zeros(TILE, F32)
            for s in range(8):
                acc = lax.select(p_loc[f][s], take(row(ref, c * 3 + n, pl.ds(s, 1)), p_lo[f]), acc)
            nodes.append(acc)
        return ends(nodes, p_is0[f], p_is1[f])

    def from_diag(ref, first, count):
        rows = ref.shape[0]
        flat = ref.reshape(rows * 8, 128)
        parts = []
        for h in range(count):
            nodes = []
            for n in range(3):
                acc = jnp.zeros(TILE, F32)
                for s in range(8):
                    got = flat[pl.ds(((first + h * 8) * 3 + n) * 8 + s, 8, stride=24), :]
                    acc = lax.select(d_hi[s], take(got, d_lo), acc)
                nodes.append(acc)
            parts.append(ends(nodes, d_is0, d_is1))
        return parts

    for f in range(3):
        aux[FACE_NODES[f][0]] = edge[f]
        aux[3 + f] = half_kappa
    for r in range(6, 24):
        aux[r] = jnp.zeros(TILE, F32)
    for r in range(45, 48):
        tab[r] = zone.astype(F32)
    slot_edge = from_slots(aux, 0)[0]
    slot_kedge = from_slots(aux, 1)[0] * slot_edge
    d_aux = from_diag(aux, 0, 1)[0][0]
    d_edge = jnp.broadcast_to(d_aux[0:1], TILE)
    d_kedge = jnp.broadcast_to(d_aux[1:2], TILE) * d_edge
    d_scale = [jnp.where(sub < 4, d_edge, d_kedge), jnp.where(sub < 6, d_kedge, 1.0)]
    kedge = [half_kappa * edge[f] for f in range(3)]

    sends = []

    def remote(src, dst, ssem, rsem, n):
        return pltpu.make_async_remote_copy(
            src_ref=src, dst_ref=dst, send_sem=ssem, recv_sem=rsem, device_id=at(*STEPS[n]), device_id_type=MESH
        )

    def part_copy(k, i, rows, a):
        return remote(
            sbuf.at[k, i, rows], rbuf.at[k, 3 - i, rows], send_sem.at[k, a + i], recv_sem.at[k, a + 3 - i], MAIN[i]
        )

    def first_copy(k, i):
        return part_copy(k, i, pl.ds(0, FIRST), 0)

    def second_copy(k, i):
        return part_copy(k, i, pl.ds(FIRST, 30 - FIRST), 8)

    def forward_copy(k, i):
        return part_copy(k, i, pl.ds(0, 20), 0)

    def diag_copy(k, i):
        return remote(
            sdiag.at[k], rdiag.at[k, 3 - i], send_sem.at[k, 4 + i], recv_sem.at[k, 7 - i], DIAG[i]
        )

    def send(make, k, table, order):
        for i in order:
            @pl.when(exists(table[i]))
            def _():
                make(k, i).start()
            sends.append((make, k, table, i))

    def arrive(make, k, table, which):
        for i in which:
            @pl.when(exists(table[i]))
            def _():
                make(k, 3 - i).wait_recv()

    def fill_slots(k, ref, comps, first_channel, scales):
        for c in comps:
            pair = from_slots(ref, c)
            for j in range(2 if c < COMPS else 1):
                value = pair[j] * scales(c) if c < COMPS and scales else pair[j]
                ch = c * 2 + j + first_channel if c < COMPS else c - COMPS
                for d in range(4):
                    sbuf[k, d, ch] = value[2 * d : 2 * d + 2]

    def unpack_state(m):
        flat = xs.at[m].reshape(42 * 8, 128)
        for s in range(8):
            flat[pl.ds(s, 42, stride=8), :] = states[m, :, s * 128 : (s + 1) * 128].astype(F32)

    def pack_diag(k, halves, scales):
        packed = jnp.zeros(TILE, F32)
        for j in range(2):
            for h in range(2):
                g = 2 * j + h
                value = halves[h][j] * scales[h] if scales else halves[h][j]
                packed = lax.select(lane16[g], pltpu.roll(value, 16 * g, axis=1) if g else value, packed)
        sdiag[k] = packed
        send(diag_copy, k, DIAG, (0, 1, 2, 3))

    def merge_diag(k):
        acc = rdiag[k, 0]
        for d in range(1, 4):
            acc = lax.select(lane4[d], rdiag[k, d], acc)
        for j in range(2):
            for h in range(2):
                g = 2 * j + h
                cdiag[k, j, h * 8 : h * 8 + 8] = pltpu.roll(acc, 128 - 16 * g, axis=1) if g else acc

    def receive(k, ref, channels, rows):
        for f in range(3):
            for ch in channels:
                acc = ref[f, ch]
                for s in rows:
                    acc = lax.select(
                        p_rem[f][s], take(row(rbuf, k, s // 2, ch, pl.ds(s % 2, 1)), p_lo[f]), acc
                    )
                ref[f, ch] = acc

    def receive_diag(k, ref, f, ch, c, j):
        return lax.select(p_rem[f][8], take(row(cdiag, k, j, pl.ds(c, 1)), p_lo[f]), ref[f, ch])

    base = 4 * (ix * GY + iy)

    def relative(ids):
        return (ids - base + (BEHIND + ZONES)) & (ZONES - 1)

    tf = jnp.zeros(TILE, F32)
    tc = jnp.zeros(TILE, F32)
    far_terms = [jnp.zeros(TILE, F32)] * 3
    weights = {2: 2.0 / 3.0, 1: 0.25, 0: 1.0}
    FWD = 3

    def own_terms(k, v, x, weight, tf, tc):
        moment = jnp.sqrt(1.0 + (1.0 / 6.0) * sum(x[r] * x[r] for r in range(3, 9)))
        acc = jnp.zeros(TILE, F32)
        for r in range(3, 9):
            acc = acc + v[r] * x[r]
        tf = tf - weight * (wet * rough * moment) * acc
        flows = jnp.zeros(TILE, F32)
        faces = jnp.zeros(TILE, F32)
        for n in range(3):
            above = v[12 + n] - 0.5 * wet * v[9 + n]
            flows = flows + above * (x[9 + n] - x[12 + n])
            acc = tab[12 + n] * x[12 + n]
            for l in range(10):
                r = 12 + l * 3 + n
                if l:
                    acc = acc + tab[r] * x[r]
                if l < 9:
                    flows = flows + (v[r + 3] - v[r]) * (x[r] - x[r + 3])
            faces = faces + sum(kedge[f] for f in range(3) if n in FACE_NODES[f]) * acc
        tc = tc + weight * (kappa * flows - faces)
        return tf, tc, wet * rough_zone * moment

    def zone_bins(tf, tc):
        bins_f = jnp.zeros(TILE, F32)
        bins_c = [jnp.zeros(TILE, F32) for _ in range(WINDOW // 8)]
        none = jnp.zeros(TILE, F32)
        own_rel = relative(zone)
        far_rel = [relative(kept[6 + f].astype(jnp.int32)) for f in range(3)]
        for s in range(8):
            rel = jnp.broadcast_to(own_rel[s : s + 1], TILE) - sub
            tf_row = jnp.broadcast_to(tf[s : s + 1], TILE)
            tc_row = jnp.broadcast_to(tc[s : s + 1], TILE)
            hit = rel == BEHIND
            bins_f = bins_f + lax.select(hit, tf_row, none)
            bins_c[BEHIND // 8] = bins_c[BEHIND // 8] + lax.select(hit, tc_row, none)
            for f in range(3):
                rel = jnp.broadcast_to(far_rel[f][s : s + 1], TILE) - sub
                term = jnp.broadcast_to(far_terms[f][s : s + 1], TILE)
                for z in (0, 1, 2, 4, 5, 6, 8, 9, 10):
                    bins_c[z] = bins_c[z] + lax.select(rel == 8 * z, term, none)
        rows = jnp.concatenate(bins_c + [bins_f] + [none] * (15 - WINDOW // 8), axis=0)
        sums = lax.dot_general(
            jnp.ones(TILE, F32), rows, (((1,), (1,)), ((), ())),
            precision=lax.Precision.HIGHEST, preferred_element_type=F32,
        )
        rel = (lane - base + (BEHIND + ZONES)) & 127
        is_friction = sub == 0
        own_zone = (rel >= BEHIND) & (rel < BEHIND + 8)
        found = take(sums, lanes_of(jnp.where(is_friction, rel + (WINDOW - BEHIND), rel) & 127))
        return jnp.where(is_friction, jnp.where(own_zone, found, 0.0), jnp.where(rel < WINDOW, found, 0.0))

    gy_copies = [
        pltpu.make_async_remote_copy(
            src_ref=gyb.at[iy], dst_ref=gyb.at[iy], send_sem=gy_send.at[d], recv_sem=gy_recv.at[d],
            device_id=at(0, d), device_id_type=MESH,
        )
        for d in (4, 3, 5, 2, 6, 1, 7)
    ]
    gx_copies = [
        pltpu.make_async_remote_copy(
            src_ref=gxb.at[ix], dst_ref=gxb.at[ix], send_sem=gx_send.at[d], recv_sem=gx_recv.at[d],
            device_id=at(d, 0), device_id_type=MESH,
        )
        for d in (8, 6, 10, 7, 9, 5, 11, 4, 12, 3, 13, 2, 14, 1, 15)
    ]

    for k in (2, 1, 0):
        v = cot if k == 2 else lam.at[k]
        weight = weights[k] * DT
        x = xs.at[k]
        if k == 2:
            unpack_state(2)
        squares = []
        for n in range(3):
            squares.append(sum(x[c * 3 + n] * x[c * 3 + n] for c in range(4)))
        q = [squares[a] + squares[b] for a, b in FACE_NODES]
        for f in range(3):
            tab[42 + FACE_NODES[f][0]] = q[f]
        wet_area = wet * area
        for r in range(12):
            tab[r] = wet_area * v[r]
        for r in range(12, 42):
            tab[r] = area * v[r]

        if k == 0:
            tf, tc, wet_friction = own_terms(k, v, x, weight, tf, tc)
            for f in range(3):
                term = jnp.zeros(TILE, F32)
                for ch in range(8, 28):
                    r = 12 + ((ch - 8) // 2) * 3 + FACE_NODES[f][ch % 2]
                    term = term + fwd[f, ch - 8] * tab[r]
                tc = tc + weight * kedge[f] * term
            gyb[iy] = zone_bins(tf, tc)[0:2]
            for copy in gy_copies:
                copy.start()

        last = ZCOMP if k == 2 else QCOMP
        if k < 2:
            pack_diag(k, from_diag(tab, 0, 2), d_scale)
        slot_scale = lambda c: slot_edge if c < 4 else slot_kedge
        fill_slots(k, tab, list(range(COMPS, last + 1)) + list(range(SPLIT)), 2, slot_scale)
        if k == 2:
            halves = from_diag(tab, 0, 2)
            pl.semaphore_wait(barrier, greeters)
            pack_diag(k, halves, d_scale)
        send(first_copy, k, MAIN, (0, 3, 1, 2))
        fill_slots(k, tab, range(SPLIT, COMPS), 2, slot_scale)
        send(second_copy, k, MAIN, (0, 3, 1, 2))

        if k == 2:
            for m in (0, 1):
                unpack_state(m)
            for small, wide, size in ((vol_ref, vol, 12), (fin_ref, fin, 8), (fout_ref, fout, 8)):
                for b in range(size):
                    for a in range(size):
                        wide[b * size + a] = jnp.broadcast_to(small[b : b + 1, a : a + 1], TILE)

        if k == 2:
            for f in range(3):
                outer_edge = from_partner(aux, 0, f)[0]
                kept[f] = outer_edge
                kept[3 + f] = from_partner(aux, 1, f)[0] * outer_edge
        for f in range(3):
            for c in range(last + 1):
                pair = from_partner(tab, c, f)
                if c < COMPS:
                    scale = kept[f] if c < 4 else kept[3 + f]
                    local[f, c * 2 + 2] = pair[0] * scale
                    local[f, c * 2 + 3] = pair[1] * scale
                else:
                    local[f, c - COMPS] = pair[0]

        if k > 0:
            tf, tc, wet_friction = own_terms(k, v, x, weight, tf, tc)
        bars = [None] * 12
        for r in range(12):
            bars[r] = sum(vol[b * 12 + r] * tab[b] for b in range(12))
            if 3 <= r < 9:
                bars[r] = bars[r] - wet_friction * v[r]
        for f in range(3):
            for a in range(8):
                total = sum(
                    fin[b * 8 + a] * tab[(b // 2) * 3 + FACE_NODES[f][b % 2]] for b in range(8)
                )
                r = (a // 2) * 3 + FACE_NODES[f][a % 2]
                bars[r] = bars[r] + edge[f] * total
        for n in range(3):
            node_edge = sum(kedge[f] for f in range(3) if n in FACE_NODES[f])
            above = v[12 + n] - 0.5 * wet * v[9 + n]
            bars[9 + n] = bars[9 + n] + kappa * above
            for l in range(10):
                r = 12 + l * 3 + n
                below = v[r + 3] - v[r] if l < 9 else 0.0
                pre[r] = kappa * (below - above) - node_edge * tab[r]
                above = below
        for r in range(12):
            pre[r] = bars[r]

        if k == 2:
            halves = from_diag(xs.at[0], 4, 1) + from_diag(xs.at[0], 6, 1)
            pack_diag(FWD, halves, None)
            fill_slots(FWD, xs.at[0], range(4, COMPS), -8, None)
            send(forward_copy, FWD, MAIN, (0, 3, 1, 2))
            for f in range(3):
                for c in range(4, COMPS):
                    pair = from_partner(xs.at[0], c, f)
                    fwd[f, c * 2 - 8] = pair[0]
                    fwd[f, c * 2 - 7] = pair[1]
        if k == 1:
            arrive(forward_copy, FWD, MAIN, range(4))
            arrive(diag_copy, FWD, DIAG, range(4))
            merge_diag(FWD)
            receive(FWD, fwd, range(20), range(8))
            for f in range(3):
                for ch in range(20):
                    c = ch // 2 if ch < 4 else ch // 2 + 6
                    fwd[f, ch] = receive_diag(FWD, fwd, f, ch, c, ch % 2)
        if k == 0:
            for copy in gy_copies:
                copy.wait_recv()
            total = gyb[0]
            for i in range(1, GY):
                total = total + gyb[i]
            gxb[ix] = total
            for copy in gx_copies:
                copy.start()

        early = [ch for ch in range(FIRST) if ch != 1 or k == 2]
        late = range(FIRST, 30)
        terms = [jnp.zeros(TILE, F32)] * 3

        def porewater(f, channels):
            for ch in channels:
                r = 12 + ((ch - 10) // 2) * 3 + FACE_NODES[f][ch % 2]
                value = receive_diag(k, local, f, ch, ch // 2 - 1, ch % 2)
                if k > 0:
                    terms[f] = terms[f] + value * x[r]
                pre[r] = pre[r] + value

        arrive(first_copy, k, MAIN, (1, 2))
        receive(k, local, early, range(2, 6))
        arrive(second_copy, k, MAIN, (1, 2))
        receive(k, local, late, range(2, 6))
        arrive(first_copy, k, MAIN, (0, 3))
        receive(k, local, early, (0, 1, 6, 7))
        arrive(diag_copy, k, DIAG, range(4))
        merge_diag(k)
        for f in range(3):
            if k == 2:
                kept[6 + f] = receive_diag(k, local, f, 1, ZCOMP, 0)
            outer_q = receive_diag(k, local, f, 0, QCOMP, 0)
            half_speed = 0.5 * jnp.sqrt(1.0 + 0.03125 * (q[f] + outer_q))
            outer = [receive_diag(k, local, f, a + 2, a // 2, a % 2) for a in range(8)]
            for a in range(8):
                r = (a // 2) * 3 + FACE_NODES[f][a % 2]
                total = half_speed * (edge[f] * tab[r] - outer[a])
                for b in range(8):
                    total = total - fout[b * 8 + a] * outer[b]
                pre[r] = pre[r] + total
            porewater(f, range(10, FIRST))
        arrive(second_copy, k, MAIN, (0, 3))
        receive(k, local, late, (0, 1, 6, 7))
        for f in range(3):
            porewater(f, late)
            far_terms[f] = far_terms[f] + weight * terms[f]

        for r in range(42):
            if k == 2:
                lam[1, r] = (2.0 / 3.0) * (cot[r] + DT * pre[r])
            elif k == 1:
                lam[0, r] = 0.25 * (lam[1, r] + DT * pre[r])
            else:
                out[r] = cot[r] * (1.0 / 3.0) + 0.75 * lam[1, r] + lam[0, r] + DT * pre[r]

    for copy in gx_copies:
        copy.wait_recv()
    lane2 = lax.broadcasted_iota(jnp.int32, (2, 128), 1)
    blocks = [jnp.zeros((2, 128), F32) for _ in range(4)]
    for i in range(GX):
        start = (4 * GY * i - BEHIND) % ZONES
        block, lane_at = start // 128, start % 128
        value = gxb[i]
        blocks[block] = blocks[block] + jnp.where(lane2 >= lane_at, value, 0.0)
        after = (block + 1) % 4
        blocks[after] = blocks[after] + jnp.where(lane2 >= lane_at, 0.0, value)
    for t in range(4):
        grads[0:1, t * 128 : (t + 1) * 128] = GRAD_WEIGHT * blocks[t][0:1]
        grads[1:2, t * 128 : (t + 1) * 128] = GRAD_WEIGHT * blocks[t][1:2] / zc_ref[t : t + 1]
    for make, k, table, i in sends:
        @pl.when(exists(table[i]))
        def _():
            make(k, i).wait_send()
    for copy in gy_copies + gx_copies:
        copy.wait_send()


def deliver(adjoint, grads, adjoint_out, grads_out, sem):
    first = pltpu.make_async_copy(adjoint, adjoint_out, sem.at[0])
    second = pltpu.make_async_copy(grads, grads_out, sem.at[1])
    first.start()
    second.start()
    first.wait()
    second.wait()


def local(
    cotangent, section_states, inverse_area, edge_length, roughness, soil_conductance, zone_friction,
    zone_conductivity, wet_mask, element_zone, send_face, send_count, face_partner, volume_matrix, flux_in, flux_out,
):
    vmem = pl.BlockSpec(memory_space=pltpu.VMEM)
    arrays = (
        cotangent.reshape(42, 8, 128),
        section_states.reshape(3, 42, 1024),
        inverse_area.reshape(8, 128),
        edge_length.reshape(3, 8, 128),
        roughness.reshape(8, 128),
        soil_conductance.reshape(8, 128),
        zone_friction.reshape(4, 128),
        zone_conductivity.reshape(4, 128),
        wet_mask.reshape(8, 128),
        element_zone.reshape(8, 128),
        send_face.reshape(8, 256),
        face_partner.reshape(3, 8, 128),
        volume_matrix,
        flux_in,
        flux_out,
    )
    adjoint, grads = pl.pallas_call(
        kernel,
        out_shape=(
            jax.ShapeDtypeStruct((42, 8, 128), F32),
            jax.ShapeDtypeStruct((2, ZONES), F32),
        ),
        in_specs=[pl.BlockSpec(memory_space=pl.ANY)] * 15,
        out_specs=(vmem, vmem),
        scratch_shapes=[
            pltpu.VMEM((42, 8, 128), F32),
            pltpu.VMEM((3, 42, 1024), jnp.bfloat16),
            pltpu.VMEM((8, 128), F32),
            pltpu.VMEM((3, 8, 128), F32),
            pltpu.VMEM((8, 128), F32),
            pltpu.VMEM((8, 128), F32),
            pltpu.VMEM((4, 128), F32),
            pltpu.VMEM((4, 128), F32),
            pltpu.VMEM((8, 128), jnp.int32),
            pltpu.VMEM((8, 128), jnp.int32),
            pltpu.VMEM((8, 256), jnp.int32),
            pltpu.VMEM((3, 8, 128), jnp.int32),
            pltpu.VMEM((12, 12), F32),
            pltpu.VMEM((8, 8), F32),
            pltpu.VMEM((8, 8), F32),
            pltpu.VMEM((144, 8, 128), F32),
            pltpu.VMEM((64, 8, 128), F32),
            pltpu.VMEM((64, 8, 128), F32),
            pltpu.VMEM((48, 8, 128), F32),
            pltpu.VMEM((24, 8, 128), F32),
            pltpu.VMEM((3, 42, 8, 128), F32),
            pltpu.VMEM((3, 30, 8, 128), F32),
            pltpu.VMEM((3, 20, 8, 128), F32),
            pltpu.VMEM((42, 8, 128), F32),
            pltpu.VMEM((2, 42, 8, 128), F32),
            pltpu.VMEM((9, 8, 128), F32),
            pltpu.VMEM((4, 4, 30, 2, 128), F32),
            pltpu.VMEM((4, 4, 30, 2, 128), F32),
            pltpu.VMEM((4, 8, 128), F32),
            pltpu.VMEM((4, 4, 8, 128), F32),
            pltpu.VMEM((4, 2, 16, 128), F32),
            pltpu.VMEM((GY, 2, 128), F32),
            pltpu.VMEM((GX, 2, 128), F32),
            pltpu.SemaphoreType.DMA((15,)),
            pltpu.SemaphoreType.DMA((4, 12)),
            pltpu.SemaphoreType.DMA((4, 12)),
            pltpu.SemaphoreType.DMA((GY,)),
            pltpu.SemaphoreType.DMA((GY,)),
            pltpu.SemaphoreType.DMA((GX,)),
            pltpu.SemaphoreType.DMA((GX,)),
        ],
        compiler_params=pltpu.CompilerParams(
            collective_id=0, has_side_effects=True, vmem_limit_bytes=32 << 20
        ),
        name="sections",
    )(*[pltpu.with_memory_space_constraint(array, pltpu.MemorySpace.HBM) for array in arrays])
    adjoint, grads = pl.pallas_call(
        deliver,
        out_shape=(
            jax.ShapeDtypeStruct((42, 8, 128), F32),
            jax.ShapeDtypeStruct((2, ZONES), F32),
        ),
        in_specs=[vmem, vmem],
        out_specs=(pl.BlockSpec(memory_space=pltpu.MemorySpace.HBM),) * 2,
        scratch_shapes=[pltpu.SemaphoreType.DMA((2,))],
        name="deliver",
    )(*[pltpu.with_memory_space_constraint(array, pltpu.MemorySpace.VMEM) for array in (adjoint, grads)])
    return adjoint.reshape(1, 1, 42, 1024), grads


def solution(mesh):
    placed = (
        P("gx", "gy", None, None),
        P(None, "gx", "gy", None, None),
        P("gx", "gy", None),
        P("gx", "gy", None, None),
        P("gx", "gy", None),
        P("gx", "gy", None),
        P(),
        P(),
        P("gx", "gy", None),
        P("gx", "gy", None),
        P("gx", "gy", None, None),
        P("gx", "gy", None),
        P("gx", "gy", None, None),
        P(),
        P(),
        P(),
    )
    return jax.shard_map(
        local,
        mesh=mesh,
        in_specs=placed,
        out_specs=(P("gx", "gy", None, None), P()),
        check_vma=False,
    )
```

```python
import jax
import jax.numpy as jnp
from jax import lax
from jax.experimental import pallas as pl
from jax.experimental.pallas import tpu as pltpu
from jax.sharding import PartitionSpec as P

GX, GY = 16, 8
COMPS = 14
QCOMP, ZCOMP = 14, 15
ZONES = 512
DT = 0.2
GRAD_WEIGHT = 1.0 / 64.0
SPLIT = 7
FIRST = 2 + 2 * SPLIT
FACE_NODES = ((1, 2), (2, 0), (0, 1))
MAIN = (1, 3, 4, 6)
DIAG = (0, 2, 5, 7)
STEPS = ((-1, -1), (-1, 0), (-1, 1), (0, -1), (0, 1), (1, -1), (1, 0), (1, 1))
WINDOW, BEHIND = 88, 40
MESH = pl.DeviceIdType.MESH
TILE = (8, 128)
F32 = jnp.float32


LOOKUP = lax.GatherDimensionNumbers(
    offset_dims=(), collapsed_slice_dims=(1,), start_index_map=(1,), operand_batching_dims=(0,),
    start_indices_batching_dims=(0,),
)


def lanes_of(idx):
    return idx.reshape(8, 128, 1)


def take(x, idx):
    return lax.gather(
        x, idx, LOOKUP, slice_sizes=(1, 1), mode=lax.GatherScatterMode.PROMISE_IN_BOUNDS
    )


def row(ref, *at):
    return jnp.broadcast_to(ref[at], TILE)


def pick(code, values, like):
    out = jnp.full(TILE, values[-1], like.dtype)
    for i in range(len(values) - 2, -1, -1):
        out = jnp.where(code == i, values[i], out)
    return out


def ends(nodes, is0, is1):
    a, b, c = nodes
    first = lax.select(is0, b, lax.select(is1, c, a))
    second = lax.select(is0, c, lax.select(is1, a, b))
    return first, second


def kernel(
    cot_hbm, states_hbm, area_hbm, edge_hbm, rough_hbm, soil_hbm, zf_hbm, zc_hbm, wet_hbm, zone_hbm, send_hbm,
    partner_hbm, vol_hbm, fin_hbm, fout_hbm,
    out, grads,
    cot, states, area_ref, edge_ref, rough_ref, soil_ref, zf_ref, zc_ref, wet_ref, zone_ref, send_ref, partner_ref,
    vol_ref, fin_ref, fout_ref, vol, fin, fout,
    tab, aux, xs, local, fwd, pre, lam, kept, sbuf, rbuf, sdiag, rdiag, cdiag, gyb, gxb,
    in_sem, send_sem, recv_sem, gy_send, gy_recv, gx_send, gx_recv,
):
    ix, iy = lax.axis_index("gx"), lax.axis_index("gy")

    def at(dx, dy):
        return (lax.rem(ix + dx + GX, GX), lax.rem(iy + dy + GY, GY))

    side_x = {-1: (ix + GX - 1) // GX, 0: 1, 1: (2 * GX - 2 - ix) // GX}
    side_y = {-1: (iy + GY - 1) // GY, 0: 1, 1: (2 * GY - 2 - iy) // GY}

    def exists(n):
        dx, dy = STEPS[n]
        return side_x[dx] * side_y[dy] == 1

    barrier = pltpu.get_barrier_semaphore()
    peers = [at(k, 0) for k in (1, 15)] + [at(0, k) for k in (1, 7)]
    peers += [at(k, 0) for k in (8, 7, 9, 6, 10, 5, 11, 4, 12, 3, 13, 2, 14)]
    peers += [at(0, k) for k in (4, 3, 5, 2, 6)]
    for n in DIAG:
        @pl.when(exists(n))
        def _():
            pl.semaphore_signal(barrier, inc=1, device_id=at(*STEPS[n]), device_id_type=MESH)
    for peer in peers:
        pl.semaphore_signal(barrier, inc=1, device_id=peer, device_id_type=MESH)
    greeters = len(peers) + (side_x[-1] + side_x[1]) * (side_y[-1] + side_y[1])

    inputs = (
        (cot_hbm, cot), (states_hbm, states), (area_hbm, area_ref), (edge_hbm, edge_ref), (rough_hbm, rough_ref),
        (soil_hbm, soil_ref), (zf_hbm, zf_ref), (zc_hbm, zc_ref), (wet_hbm, wet_ref), (zone_hbm, zone_ref),
        (send_hbm, send_ref), (partner_hbm, partner_ref), (vol_hbm, vol_ref), (fin_hbm, fin_ref), (fout_hbm, fout_ref),
    )
    reads = [pltpu.make_async_copy(src, dst, in_sem.at[i]) for i, (src, dst) in enumerate(inputs)]
    for read in reads:
        read.start()
    for read in reads:
        read.wait()

    sub = lax.broadcasted_iota(jnp.int32, TILE, 0)
    lane = lax.broadcasted_iota(jnp.int32, TILE, 1)

    lane16 = [(lane >> 4) == g for g in range(4)]
    lane4 = [((lane >> 2) & 3) == d for d in range(4)]
    area = area_ref[...]
    rough = rough_ref[...]
    wet = wet_ref[...].astype(F32)
    zone = zone_ref[...]
    edge = [edge_ref[f] for f in range(3)]
    kappa = jnp.zeros(TILE, F32)
    zfric = jnp.zeros(TILE, F32)
    zlane, zhi = lanes_of(zone & 127), zone >> 7
    for t in range(4):
        kappa = jnp.where(zhi == t, take(row(zc_ref, pl.ds(t, 1)), zlane), kappa)
        zfric = jnp.where(zhi == t, take(row(zf_ref, pl.ds(t, 1)), zlane), zfric)
    kappa = kappa * soil_ref[...]
    half_kappa = 0.5 * kappa
    rough_zone = zfric * rough

    slots = jnp.concatenate(
        [send_ref[n : n + 1, h * 128 : (h + 1) * 128] for n in MAIN for h in range(2)], axis=0
    )
    m_lo, m_f = lanes_of(slots & 127), slots >> 10
    m_hi = [((slots >> 7) & 7) == t for t in range(8)]
    m_is0, m_is1 = m_f == 0, m_f == 1
    dslots = jnp.zeros(TILE, jnp.int32)
    for i, n in enumerate(DIAG):
        first = jnp.broadcast_to(send_ref[n : n + 1, 0:128], TILE)
        d = 3 - i
        moved = pltpu.roll(first, 4 * d, axis=1) if d else first
        dslots = jnp.where((lane >> 2) == d, moved, dslots)
    d_lo, d_f = lanes_of(dslots & 127), dslots >> 10
    d_hi = [((dslots >> 7) & 7) == t for t in range(8)]
    d_is0, d_is1 = d_f == 0, d_f == 1

    p_lo, p_loc, p_rem, p_is0, p_is1 = [], [], [], [], []
    for f in range(3):
        p = partner_ref[f]
        there = p - 3072
        n = there >> 8
        slot_row = pick(n, (8, 0, 8, 2, 4, 8, 6, 8), p) + ((there >> 7) & 1)
        is_diag = (n == 0) | (n == 2) | (n == 5) | (n == 7)
        far = p >= 3072
        d_lane = pick(n, (0, 0, 4, 0, 0, 8, 0, 12), p) + (p & 3)
        p_lo.append(lanes_of(jnp.where(far & is_diag, d_lane, p & 127)))
        chunk = jnp.where(far, -1, (p >> 7) & 7)
        p_loc.append([chunk == t for t in range(8)])
        chunk = jnp.where(far, jnp.where(is_diag, 8, slot_row), -1)
        p_rem.append([chunk == t for t in range(9)])
        p_is0.append((p >> 10) == 0)
        p_is1.append((p >> 10) == 1)

    def from_slots(ref, c):
        nodes = []
        for n in range(3):
            acc = jnp.zeros(TILE, F32)
            for s in range(8):
                acc = lax.select(m_hi[s], take(row(ref, c * 3 + n, pl.ds(s, 1)), m_lo), acc)
            nodes.append(acc)
        return ends(nodes, m_is0, m_is1)

    def from_partner(ref, c, f):
        nodes = []
        for n in range(3):
            acc = jnp.zeros(TILE, F32)
            for s in range(8):
                acc = lax.select(p_loc[f][s], take(row(ref, c * 3 + n, pl.ds(s, 1)), p_lo[f]), acc)
            nodes.append(acc)
        return ends(nodes, p_is0[f], p_is1[f])

    def from_diag(ref, first, count):
        rows = ref.shape[0]
        flat = ref.reshape(rows * 8, 128)
        parts = []
        for h in range(count):
            nodes = []
            for n in range(3):
                acc = jnp.zeros(TILE, F32)
                for s in range(8):
                    got = flat[pl.ds(((first + h * 8) * 3 + n) * 8 + s, 8, stride=24), :]
                    acc = lax.select(d_hi[s], take(got, d_lo), acc)
                nodes.append(acc)
            parts.append(ends(nodes, d_is0, d_is1))
        return parts

    for f in range(3):
        aux[FACE_NODES[f][0]] = edge[f]
        aux[3 + f] = half_kappa
    for r in range(6, 24):
        aux[r] = jnp.zeros(TILE, F32)
    for r in range(45, 48):
        tab[r] = zone.astype(F32)
    slot_edge = from_slots(aux, 0)[0]
    slot_kedge = from_slots(aux, 1)[0] * slot_edge
    d_aux = from_diag(aux, 0, 1)[0][0]
    d_edge = jnp.broadcast_to(d_aux[0:1], TILE)
    d_kedge = jnp.broadcast_to(d_aux[1:2], TILE) * d_edge
    d_scale = [jnp.where(sub < 4, d_edge, d_kedge), jnp.where(sub < 6, d_kedge, 1.0)]
    kedge = [half_kappa * edge[f] for f in range(3)]

    sends = []

    def remote(src, dst, ssem, rsem, n):
        return pltpu.make_async_remote_copy(
            src_ref=src, dst_ref=dst, send_sem=ssem, recv_sem=rsem, device_id=at(*STEPS[n]), device_id_type=MESH
        )

    def part_copy(k, i, rows, a):
        return remote(
            sbuf.at[k, i, rows], rbuf.at[k, 3 - i, rows], send_sem.at[k, a + i], recv_sem.at[k, a + 3 - i], MAIN[i]
        )

    def first_copy(k, i):
        return part_copy(k, i, pl.ds(0, FIRST), 0)

    def second_copy(k, i):
        return part_copy(k, i, pl.ds(FIRST, 30 - FIRST), 8)

    def forward_copy(k, i):
        return part_copy(k, i, pl.ds(0, 20), 0)

    def diag_copy(k, i):
        return remote(
            sdiag.at[k], rdiag.at[k, 3 - i], send_sem.at[k, 4 + i], recv_sem.at[k, 7 - i], DIAG[i]
        )

    def send(make, k, table, order):
        for i in order:
            @pl.when(exists(table[i]))
            def _():
                make(k, i).start()
            sends.append((make, k, table, i))

    def arrive(make, k, table, which):
        for i in which:
            @pl.when(exists(table[i]))
            def _():
                make(k, 3 - i).wait_recv()

    def fill_slots(k, ref, comps, first_channel, scales):
        for c in comps:
            pair = from_slots(ref, c)
            for j in range(2 if c < COMPS else 1):
                value = pair[j] * scales(c) if c < COMPS and scales else pair[j]
                ch = c * 2 + j + first_channel if c < COMPS else c - COMPS
                for d in range(4):
                    sbuf[k, d, ch] = value[2 * d : 2 * d + 2]

    def unpack_state(m):
        flat = xs.at[m].reshape(42 * 8, 128)
        for s in range(8):
            flat[pl.ds(s, 42, stride=8), :] = states[m, :, s * 128 : (s + 1) * 128].astype(F32)

    def pack_diag(k, halves, scales):
        packed = jnp.zeros(TILE, F32)
        for j in range(2):
            for h in range(2):
                g = 2 * j + h
                value = halves[h][j] * scales[h] if scales else halves[h][j]
                packed = lax.select(lane16[g], pltpu.roll(value, 16 * g, axis=1) if g else value, packed)
        sdiag[k] = packed
        send(diag_copy, k, DIAG, (0, 1, 2, 3))

    def merge_diag(k):
        acc = rdiag[k, 0]
        for d in range(1, 4):
            acc = lax.select(lane4[d], rdiag[k, d], acc)
        for j in range(2):
            for h in range(2):
                g = 2 * j + h
                cdiag[k, j, h * 8 : h * 8 + 8] = pltpu.roll(acc, 128 - 16 * g, axis=1) if g else acc

    def receive(k, ref, channels, rows):
        for f in range(3):
            for ch in channels:
                acc = ref[f, ch]
                for s in rows:
                    acc = lax.select(
                        p_rem[f][s], take(row(rbuf, k, s // 2, ch, pl.ds(s % 2, 1)), p_lo[f]), acc
                    )
                ref[f, ch] = acc

    def receive_diag(k, ref, f, ch, c, j):
        return lax.select(p_rem[f][8], take(row(cdiag, k, j, pl.ds(c, 1)), p_lo[f]), ref[f, ch])

    base = 4 * (ix * GY + iy)

    def relative(ids):
        return (ids - base + (BEHIND + ZONES)) & (ZONES - 1)

    tf = jnp.zeros(TILE, F32)
    tc = jnp.zeros(TILE, F32)
    far_terms = [jnp.zeros(TILE, F32)] * 3
    weights = {2: 2.0 / 3.0, 1: 0.25, 0: 1.0}
    FWD = 3

    def own_terms(k, v, x, weight, tf, tc):
        moment = jnp.sqrt(1.0 + (1.0 / 6.0) * sum(x[r] * x[r] for r in range(3, 9)))
        acc = jnp.zeros(TILE, F32)
        for r in range(3, 9):
            acc = acc + v[r] * x[r]
        tf = tf - weight * (wet * rough * moment) * acc
        flows = jnp.zeros(TILE, F32)
        faces = jnp.zeros(TILE, F32)
        for n in range(3):
            above = v[12 + n] - 0.5 * wet * v[9 + n]
            flows = flows + above * (x[9 + n] - x[12 + n])
            acc = tab[12 + n] * x[12 + n]
            for l in range(10):
                r = 12 + l * 3 + n
                if l:
                    acc = acc + tab[r] * x[r]
                if l < 9:
                    flows = flows + (v[r + 3] - v[r]) * (x[r] - x[r + 3])
            faces = faces + sum(kedge[f] for f in range(3) if n in FACE_NODES[f]) * acc
        tc = tc + weight * (kappa * flows - faces)
        return tf, tc, wet * rough_zone * moment

    def zone_bins(tf, tc):
        bins_f = jnp.zeros(TILE, F32)
        bins_c = [jnp.zeros(TILE, F32) for _ in range(WINDOW // 8)]
        none = jnp.zeros(TILE, F32)
        own_rel = relative(zone)
        far_rel = [relative(kept[6 + f].astype(jnp.int32)) for f in range(3)]
        for s in range(8):
            rel = jnp.broadcast_to(own_rel[s : s + 1], TILE) - sub
            tf_row = jnp.broadcast_to(tf[s : s + 1], TILE)
            tc_row = jnp.broadcast_to(tc[s : s + 1], TILE)
            hit = rel == BEHIND
            bins_f = bins_f + lax.select(hit, tf_row, none)
            bins_c[BEHIND // 8] = bins_c[BEHIND // 8] + lax.select(hit, tc_row, none)
            for f in range(3):
                rel = jnp.broadcast_to(far_rel[f][s : s + 1], TILE) - sub
                term = jnp.broadcast_to(far_terms[f][s : s + 1], TILE)
                for z in (0, 1, 2, 4, 5, 6, 8, 9, 10):
                    bins_c[z] = bins_c[z] + lax.select(rel == 8 * z, term, none)
        rows = jnp.concatenate(bins_c + [bins_f] + [none] * (15 - WINDOW // 8), axis=0)
        sums = lax.dot_general(
            jnp.ones(TILE, F32), rows, (((1,), (1,)), ((), ())),
            precision=lax.Precision.HIGHEST, preferred_element_type=F32,
        )
        rel = (lane - base + (BEHIND + ZONES)) & 127
        is_friction = sub == 0
        own_zone = (rel >= BEHIND) & (rel < BEHIND + 8)
        found = take(sums, lanes_of(jnp.where(is_friction, rel + (WINDOW - BEHIND), rel) & 127))
        return jnp.where(is_friction, jnp.where(own_zone, found, 0.0), jnp.where(rel < WINDOW, found, 0.0))

    gy_copies = [
        pltpu.make_async_remote_copy(
            src_ref=gyb.at[iy], dst_ref=gyb.at[iy], send_sem=gy_send.at[d], recv_sem=gy_recv.at[d],
            device_id=at(0, d), device_id_type=MESH,
        )
        for d in (4, 3, 5, 2, 6, 1, 7)
    ]
    gx_copies = [
        pltpu.make_async_remote_copy(
            src_ref=gxb.at[ix], dst_ref=gxb.at[ix], send_sem=gx_send.at[d], recv_sem=gx_recv.at[d],
            device_id=at(d, 0), device_id_type=MESH,
        )
        for d in (8, 6, 10, 7, 9, 5, 11, 4, 12, 3, 13, 2, 14, 1, 15)
    ]

    for k in (2, 1, 0):
        v = cot if k == 2 else lam.at[k]
        weight = weights[k] * DT
        x = xs.at[k]
        if k == 2:
            unpack_state(2)
        squares = []
        for n in range(3):
            squares.append(sum(x[c * 3 + n] * x[c * 3 + n] for c in range(4)))
        q = [squares[a] + squares[b] for a, b in FACE_NODES]
        for f in range(3):
            tab[42 + FACE_NODES[f][0]] = q[f]
        wet_area = wet * area
        for r in range(12):
            tab[r] = wet_area * v[r]
        for r in range(12, 42):
            tab[r] = area * v[r]

        if k == 0:
            tf, tc, wet_friction = own_terms(k, v, x, weight, tf, tc)
            for f in range(3):
                term = jnp.zeros(TILE, F32)
                for ch in range(8, 28):
                    r = 12 + ((ch - 8) // 2) * 3 + FACE_NODES[f][ch % 2]
                    term = term + fwd[f, ch - 8] * tab[r]
                tc = tc + weight * kedge[f] * term
            gyb[iy] = zone_bins(tf, tc)[0:2]
            for copy in gy_copies:
                copy.start()

        last = ZCOMP if k == 2 else QCOMP
        if k < 2:
            pack_diag(k, from_diag(tab, 0, 2), d_scale)
        slot_scale = lambda c: slot_edge if c < 4 else slot_kedge
        fill_slots(k, tab, list(range(COMPS, last + 1)) + list(range(SPLIT)), 2, slot_scale)
        if k == 2:
            halves = from_diag(tab, 0, 2)
            pl.semaphore_wait(barrier, greeters)
            pack_diag(k, halves, d_scale)
        send(first_copy, k, MAIN, (0, 3, 1, 2))
        fill_slots(k, tab, range(SPLIT, COMPS), 2, slot_scale)
        send(second_copy, k, MAIN, (0, 3, 1, 2))

        if k == 2:
            for m in (0, 1):
                unpack_state(m)
            for small, wide, size in ((vol_ref, vol, 12), (fin_ref, fin, 8), (fout_ref, fout, 8)):
                for b in range(size):
                    for a in range(size):
                        wide[b * size + a] = jnp.broadcast_to(small[b : b + 1, a : a + 1], TILE)

        if k == 2:
            for f in range(3):
                outer_edge = from_partner(aux, 0, f)[0]
                kept[f] = outer_edge
                kept[3 + f] = from_partner(aux, 1, f)[0] * outer_edge
        for f in range(3):
            for c in range(last + 1):
                pair = from_partner(tab, c, f)
                if c < COMPS:
                    scale = kept[f] if c < 4 else kept[3 + f]
                    local[f, c * 2 + 2] = pair[0] * scale
                    local[f, c * 2 + 3] = pair[1] * scale
                else:
                    local[f, c - COMPS] = pair[0]

        if k > 0:
            tf, tc, wet_friction = own_terms(k, v, x, weight, tf, tc)
        bars = [None] * 12
        for r in range(12):
            bars[r] = sum(vol[b * 12 + r] * tab[b] for b in range(12))
            if 3 <= r < 9:
                bars[r] = bars[r] - wet_friction * v[r]
        for f in range(3):
            for a in range(8):
                total = sum(
                    fin[b * 8 + a] * tab[(b // 2) * 3 + FACE_NODES[f][b % 2]] for b in range(8)
                )
                r = (a // 2) * 3 + FACE_NODES[f][a % 2]
                bars[r] = bars[r] + edge[f] * total
        for n in range(3):
            node_edge = sum(kedge[f] for f in range(3) if n in FACE_NODES[f])
            above = v[12 + n] - 0.5 * wet * v[9 + n]
            bars[9 + n] = bars[9 + n] + kappa * above
            for l in range(10):
                r = 12 + l * 3 + n
                below = v[r + 3] - v[r] if l < 9 else 0.0
                pre[r] = kappa * (below - above) - node_edge * tab[r]
                above = below
        for r in range(12):
            pre[r] = bars[r]

        if k == 2:
            halves = from_diag(xs.at[0], 4, 1) + from_diag(xs.at[0], 6, 1)
            pack_diag(FWD, halves, None)
            fill_slots(FWD, xs.at[0], range(4, COMPS), -8, None)
            send(forward_copy, FWD, MAIN, (0, 3, 1, 2))
            for f in range(3):
                for c in range(4, COMPS):
                    pair = from_partner(xs.at[0], c, f)
                    fwd[f, c * 2 - 8] = pair[0]
                    fwd[f, c * 2 - 7] = pair[1]
        if k == 1:
            arrive(forward_copy, FWD, MAIN, range(4))
            arrive(diag_copy, FWD, DIAG, range(4))
            merge_diag(FWD)
            receive(FWD, fwd, range(20), range(8))
            for f in range(3):
                for ch in range(20):
                    c = ch // 2 if ch < 4 else ch // 2 + 6
                    fwd[f, ch] = receive_diag(FWD, fwd, f, ch, c, ch % 2)
        if k == 0:
            for copy in gy_copies:
                copy.wait_recv()
            total = gyb[0]
            for i in range(1, GY):
                total = total + gyb[i]
            gxb[ix] = total
            for copy in gx_copies:
                copy.start()

        early = [ch for ch in range(FIRST) if ch != 1 or k == 2]
        late = range(FIRST, 30)
        terms = [jnp.zeros(TILE, F32)] * 3

        def porewater(f, channels):
            for ch in channels:
                r = 12 + ((ch - 10) // 2) * 3 + FACE_NODES[f][ch % 2]
                value = receive_diag(k, local, f, ch, ch // 2 - 1, ch % 2)
                if k > 0:
                    terms[f] = terms[f] + value * x[r]
                pre[r] = pre[r] + value

        arrive(first_copy, k, MAIN, (1, 2))
        receive(k, local, early, range(2, 6))
        arrive(second_copy, k, MAIN, (1, 2))
        receive(k, local, late, range(2, 6))
        arrive(first_copy, k, MAIN, (0, 3))
        receive(k, local, early, (0, 1, 6, 7))
        arrive(diag_copy, k, DIAG, range(4))
        merge_diag(k)
        for f in range(3):
            if k == 2:
                kept[6 + f] = receive_diag(k, local, f, 1, ZCOMP, 0)
            outer_q = receive_diag(k, local, f, 0, QCOMP, 0)
            half_speed = 0.5 * jnp.sqrt(1.0 + 0.03125 * (q[f] + outer_q))
            outer = [receive_diag(k, local, f, a + 2, a // 2, a % 2) for a in range(8)]
            for a in range(8):
                r = (a // 2) * 3 + FACE_NODES[f][a % 2]
                total = half_speed * (edge[f] * tab[r] - outer[a])
                for b in range(8):
                    total = total - fout[b * 8 + a] * outer[b]
                pre[r] = pre[r] + total
            porewater(f, range(10, FIRST))
        arrive(second_copy, k, MAIN, (0, 3))
        receive(k, local, late, (0, 1, 6, 7))
        for f in range(3):
            porewater(f, late)
            far_terms[f] = far_terms[f] + weight * terms[f]

        for r in range(42):
            if k == 2:
                lam[1, r] = (2.0 / 3.0) * (cot[r] + DT * pre[r])
            elif k == 1:
                lam[0, r] = 0.25 * (lam[1, r] + DT * pre[r])
            else:
                out[r] = cot[r] * (1.0 / 3.0) + 0.75 * lam[1, r] + lam[0, r] + DT * pre[r]

    for copy in gx_copies:
        copy.wait_recv()
    lane2 = lax.broadcasted_iota(jnp.int32, (2, 128), 1)
    blocks = [jnp.zeros((2, 128), F32) for _ in range(4)]
    for i in range(GX):
        start = (4 * GY * i - BEHIND) % ZONES
        block, lane_at = start // 128, start % 128
        value = gxb[i]
        blocks[block] = blocks[block] + jnp.where(lane2 >= lane_at, value, 0.0)
        after = (block + 1) % 4
        blocks[after] = blocks[after] + jnp.where(lane2 >= lane_at, 0.0, value)
    for t in range(4):
        grads[0:1, t * 128 : (t + 1) * 128] = GRAD_WEIGHT * blocks[t][0:1]
        grads[1:2, t * 128 : (t + 1) * 128] = GRAD_WEIGHT * blocks[t][1:2] / zc_ref[t : t + 1]
    for make, k, table, i in sends:
        @pl.when(exists(table[i]))
        def _():
            make(k, i).wait_send()
    for copy in gy_copies + gx_copies:
        copy.wait_send()


def deliver(adjoint, grads, adjoint_out, grads_out, sem):
    first = pltpu.make_async_copy(adjoint, adjoint_out, sem.at[0])
    second = pltpu.make_async_copy(grads, grads_out, sem.at[1])
    first.start()
    second.start()
    first.wait()
    second.wait()


def local(
    cotangent, section_states, inverse_area, edge_length, roughness, soil_conductance, zone_friction,
    zone_conductivity, wet_mask, element_zone, send_face, send_count, face_partner, volume_matrix, flux_in, flux_out,
):
    vmem = pl.BlockSpec(memory_space=pltpu.VMEM)
    arrays = (
        cotangent.reshape(42, 8, 128),
        section_states.reshape(3, 42, 1024),
        inverse_area.reshape(8, 128),
        edge_length.reshape(3, 8, 128),
        roughness.reshape(8, 128),
        soil_conductance.reshape(8, 128),
        zone_friction.reshape(4, 128),
        zone_conductivity.reshape(4, 128),
        wet_mask.reshape(8, 128),
        element_zone.reshape(8, 128),
        send_face.reshape(8, 256),
        face_partner.reshape(3, 8, 128),
        volume_matrix,
        flux_in,
        flux_out,
    )
    adjoint, grads = pl.pallas_call(
        kernel,
        out_shape=(
            jax.ShapeDtypeStruct((42, 8, 128), F32),
            jax.ShapeDtypeStruct((2, ZONES), F32),
        ),
        in_specs=[pl.BlockSpec(memory_space=pl.ANY)] * 15,
        out_specs=(vmem, vmem),
        scratch_shapes=[
            pltpu.VMEM((42, 8, 128), F32),
            pltpu.VMEM((3, 42, 1024), jnp.bfloat16),
            pltpu.VMEM((8, 128), F32),
            pltpu.VMEM((3, 8, 128), F32),
            pltpu.VMEM((8, 128), F32),
            pltpu.VMEM((8, 128), F32),
            pltpu.VMEM((4, 128), F32),
            pltpu.VMEM((4, 128), F32),
            pltpu.VMEM((8, 128), jnp.int32),
            pltpu.VMEM((8, 128), jnp.int32),
            pltpu.VMEM((8, 256), jnp.int32),
            pltpu.VMEM((3, 8, 128), jnp.int32),
            pltpu.VMEM((12, 12), F32),
            pltpu.VMEM((8, 8), F32),
            pltpu.VMEM((8, 8), F32),
            pltpu.VMEM((144, 8, 128), F32),
            pltpu.VMEM((64, 8, 128), F32),
            pltpu.VMEM((64, 8, 128), F32),
            pltpu.VMEM((48, 8, 128), F32),
            pltpu.VMEM((24, 8, 128), F32),
            pltpu.VMEM((4, 42, 8, 128), F32),
            pltpu.VMEM((3, 30, 8, 128), F32),
            pltpu.VMEM((3, 20, 8, 128), F32),
            pltpu.VMEM((42, 8, 128), F32),
            pltpu.VMEM((2, 42, 8, 128), F32),
            pltpu.VMEM((9, 8, 128), F32),
            pltpu.VMEM((4, 4, 30, 2, 128), F32),
            pltpu.VMEM((4, 4, 30, 2, 128), F32),
            pltpu.VMEM((4, 8, 128), F32),
            pltpu.VMEM((4, 4, 8, 128), F32),
            pltpu.VMEM((4, 2, 16, 128), F32),
            pltpu.VMEM((GY, 2, 128), F32),
            pltpu.VMEM((GX, 2, 128), F32),
            pltpu.SemaphoreType.DMA((15,)),
            pltpu.SemaphoreType.DMA((4, 12)),
            pltpu.SemaphoreType.DMA((4, 12)),
            pltpu.SemaphoreType.DMA((GY,)),
            pltpu.SemaphoreType.DMA((GY,)),
            pltpu.SemaphoreType.DMA((GX,)),
            pltpu.SemaphoreType.DMA((GX,)),
        ],
        compiler_params=pltpu.CompilerParams(
            collective_id=0, has_side_effects=True, vmem_limit_bytes=32 << 20
        ),
        name="sections",
    )(*[pltpu.with_memory_space_constraint(array, pltpu.MemorySpace.HBM) for array in arrays])
    adjoint, grads = pl.pallas_call(
        deliver,
        out_shape=(
            jax.ShapeDtypeStruct((42, 8, 128), F32),
            jax.ShapeDtypeStruct((2, ZONES), F32),
        ),
        in_specs=[vmem, vmem],
        out_specs=(pl.BlockSpec(memory_space=pltpu.MemorySpace.HBM),) * 2,
        scratch_shapes=[pltpu.SemaphoreType.DMA((2,))],
        name="deliver",
    )(*[pltpu.with_memory_space_constraint(array, pltpu.MemorySpace.VMEM) for array in (adjoint, grads)])
    return adjoint.reshape(1, 1, 42, 1024), grads


def solution(mesh):
    placed = (
        P("gx", "gy", None, None),
        P(None, "gx", "gy", None, None),
        P("gx", "gy", None),
        P("gx", "gy", None, None),
        P("gx", "gy", None),
        P("gx", "gy", None),
        P(),
        P(),
        P("gx", "gy", None),
        P("gx", "gy", None),
        P("gx", "gy", None, None),
        P("gx", "gy", None),
        P("gx", "gy", None, None),
        P(),
        P(),
        P(),
    )
    return jax.shard_map(
        local,
        mesh=mesh,
        in_specs=placed,
        out_specs=(P("gx", "gy", None, None), P()),
        check_vma=False,
    )
```
